512 devices in a mesh: group: 16 (over x, y_lo, core), shard: 32 (over y_hi, z).
Axes of the slice: x: 4, y: 8 (y_hi: 4, y_lo: 2; y = y_hi * 2 + y_lo), z: 8, core: 2. Of those that a mesh axis runs over, the one named last changes fastest.
Arguments:
- hidden: bfloat16 [8192, 8192], P('group', 'shard'), may hold values from -6 to 6
- w_x: bfloat16 [8192, 8192], P('group', 'shard'), may hold values from -0.0625 to 0.0625
- w_small: bfloat16 [8192, 2176], P('shard'), may hold values from -0.0625 to 0.0625
- conv_x: float32 [4, 8192], P(None, 'shard'), may hold values from -3 to 3
- conv_x_bias: float32 [8192], P('shard'), may hold values from -2 to 2
- conv_bc: float32 [4, 2048], replicated, may hold values from -1.5 to 1.5
- conv_bc_bias: float32 [2048], replicated, may hold values from -1 to 1
- rate: float32 [128], P('shard'), may hold values from 0.002 to 0.06
- dt_bias: float32 [128], P('shard'), may hold values from -2 to 0.5
- dskip: float32 [128], P('shard'), may hold values from 0.5 to 1.5
- old_state: float32 [64, 128, 64, 256], P('group', 'shard'), may hold values from -2 to 2
- x_tail: float32 [64, 3, 8192], P('group', None, 'shard'), may hold values from -6 to 6
- bc_tail: float32 [64, 3, 2048], P('group'), may hold values from -6 to 6
- req_count: int32 [16], replicated, may hold values from 1 to 4, as said below
- req_source: int32 [16, 4], replicated, may hold values from 0 to 63, as said below
- req_start: int32 [16, 4], replicated, may hold values from 0 to 512, as said below
Outputs:
- y_out: bfloat16 [8192, 8192], P('group', 'shard')
- new_state: float32 [64, 128, 64, 256], P('group', 'shard')
The draws below stay inside these ranges and needn't reach their ends.
Inputs may be any that keep to these rules, and one draw needn't show every extreme that they name: `req_count`: some group serves 4 requests. `req_source`: every place is named by exactly one entry; the places named by one group lie in distinct groups, so one group takes at most one request from any one group's places. `req_start`: each group's row starts with 0 and rises strictly over its first req_count entries; later entries equal 512.
All inputs are finite; a program needn't handle non-finite values.
Results may differ from the reference program's by a relative error of at most 0.006.
Values may be sent and summed in bfloat16 or wider, within the bound.
No kernel may reach another device: no remote copies, remote signals or barrier semaphores. Data moves between devices by JAX's collectives and lax.ppermute only.
A program may use at most 128 MiB of HBM per device.

```python
import math
import jax
import jax.numpy as jnp
from jax import lax

D = 8192
P_SIZE = 64
DSTATE = 256
KCONV = 4
NGRP = 4
TOK_GRP = 512
REQ_GRP = 4
HEADS = 128
GROUPS = 16
SLOTS = 64
TOKENS = 8192


def request_plan(key):
    base_key = jax.random.fold_in(key, 7101)
    split_keys = jax.random.split(base_key, 6)
    counts = jax.random.randint(split_keys[0], (GROUPS,), 1, REQ_GRP + 1)
    fullest = jax.random.randint(split_keys[1], (), 0, GROUPS)
    counts = jnp.where(jnp.arange(GROUPS) == fullest, REQ_GRP, counts).astype(jnp.int32)

    def group_starts(sub_key, used_count):
        chosen = jax.random.permutation(sub_key, TOK_GRP - 1)[:REQ_GRP - 1] + 1
        chosen = jnp.sort(chosen).astype(jnp.int32)
        starts = jnp.concatenate([jnp.zeros((1,), jnp.int32), chosen])
        slot_ids = jnp.arange(REQ_GRP)
        return jnp.where(slot_ids < used_count, starts, TOK_GRP).astype(jnp.int32)
    starts = jax.vmap(group_starts)(jax.random.split(split_keys[2], GROUPS), counts)
    order_one = jax.random.permutation(split_keys[3], GROUPS)
    order_two = jax.random.permutation(split_keys[4], GROUPS)
    shifts = jax.random.permutation(split_keys[5], GROUPS)[:REQ_GRP]
    home_groups = order_one[(order_two[:, None] + shifts[None, :]) % GROUPS]
    sources = (home_groups * REQ_GRP + jnp.arange(REQ_GRP)[None, :]).astype(jnp.int32)
    return (counts, sources, starts)


def draw_req_count(key, part):
    return request_plan(key)[0]


def draw_req_source(key, part):
    return request_plan(key)[1]


def draw_req_start(key, part):
    return request_plan(key)[2]


def shard_levels(stream_key, dims, cuts, smallest, high):
    def one(dim, blocks):
        draws = jax.random.uniform(jax.random.fold_in(jax.random.fold_in(stream_key, 6), dim), (blocks,), jnp.float32, smallest / len(cuts), high / len(cuts))
        return jnp.repeat(jnp.exp(draws), dims[dim] // blocks).reshape((-1,) + (1,) * (len(dims) - dim - 1))

    factor_of = one(*cuts[0])
    for cut in cuts[1:]:
        factor_of = factor_of * one(*cut)
    return factor_of


def noise(stream_key, shape, scale, most, pieces=(), kind=jnp.bfloat16):
    level = shard_levels(stream_key, shape, pieces, -0.22, 0.18) if pieces else 1.0
    result = jax.random.normal(stream_key, shape, jnp.float32) * scale * level
    return jnp.minimum(jnp.maximum(result, -most), most).astype(kind)


def setup_inputs(seed: int = 0) -> dict:
    keys = jax.random.split(jax.random.key(seed), 17)
    hidden = noise(keys[0], (TOKENS, D), 1.0, 6.0, ((0, 16), (1, 32)))
    w_x = noise(keys[1], (D, HEADS * P_SIZE), D ** -0.5, 0.0625, ((0, 16), (1, 32)))
    w_small = noise(keys[2], (D, 2 * NGRP * DSTATE + HEADS), D ** -0.5, 0.0625, ((0, 32),))
    conv_x = noise(keys[3], (KCONV, HEADS * P_SIZE), KCONV ** -0.5, 3.0, ((1, 32),), jnp.float32)
    conv_x_bias = noise(keys[4], (HEADS * P_SIZE,), 0.3, 2.0, ((0, 32),), jnp.float32)
    conv_bc = noise(keys[5], (KCONV, 2 * NGRP * DSTATE), 16 ** -0.5, 1.5, (), jnp.float32)
    conv_bc_bias = noise(keys[6], (2 * NGRP * DSTATE,), 0.2, 1.0, (), jnp.float32)
    rate = jnp.clip(jnp.exp(math.log(0.06) - 3.4011973 * jax.random.uniform(keys[7], (HEADS,), jnp.float32) ** shard_levels(keys[7], (HEADS,), ((0, 32),), -0.2, 0.2)), 0.002, 0.06)
    dt_bias = jnp.clip(-2.0 + 2.5 * jax.random.uniform(keys[8], (HEADS,), jnp.float32) ** shard_levels(keys[8], (HEADS,), ((0, 32),), -0.2, 0.2), -2.0, 0.5)
    dskip = jnp.clip(0.5 + 1.0 * jax.random.uniform(keys[9], (HEADS,), jnp.float32) ** shard_levels(keys[9], (HEADS,), ((0, 32),), -0.2, 0.2), 0.5, 1.5)
    old_state = noise(keys[10], (SLOTS, HEADS, P_SIZE, DSTATE), 0.3, 2.0, ((0, 16), (1, 32)), jnp.float32)
    x_tail = noise(keys[11], (SLOTS, KCONV - 1, HEADS * P_SIZE), 1.0, 6.0, ((0, 16), (2, 32)), jnp.float32)
    bc_tail = noise(keys[12], (SLOTS, KCONV - 1, 2 * NGRP * DSTATE), 1.0, 6.0, ((0, 16),), jnp.float32)
    req_count = draw_req_count(jax.random.fold_in(keys[16], 71), 0)
    req_source = draw_req_source(jax.random.fold_in(keys[16], 71), 0)
    req_start = draw_req_start(jax.random.fold_in(keys[16], 71), 0)
    return dict(hidden=hidden, w_x=w_x, w_small=w_small, conv_x=conv_x, conv_x_bias=conv_x_bias, conv_bc=conv_bc, conv_bc_bias=conv_bc_bias, rate=rate, dt_bias=dt_bias, dskip=dskip, old_state=old_state, x_tail=x_tail, bc_tail=bc_tail, req_count=req_count, req_source=req_source, req_start=req_start)


highest_mode = lax.Precision.HIGHEST


def token_requests(starts, length):
    positions = jnp.arange(length, dtype=jnp.int32)
    return (jnp.sum((starts[None, :] <= positions[:, None]).astype(jnp.int32), axis=1) - 1).astype(jnp.int32)


def causal_conv(signal, tail_vals, starts, req_tok, kernel, shift_bias):
    length = signal.shape[0]
    positions = jnp.arange(length, dtype=jnp.int32)
    own_start = jnp.take(starts, req_tok)
    tok_tail = jnp.take(tail_vals, req_tok, axis=0)
    values = signal.astype(jnp.float32)
    summed = kernel[KCONV - 1] * values
    tail_index = jnp.arange(KCONV - 1, dtype=jnp.int32)
    for lag_steps in range(1, KCONV):
        shifted = jnp.concatenate([jnp.zeros((lag_steps, values.shape[1]), jnp.float32), values[:-lag_steps]], axis=0)
        before = own_start - (positions - lag_steps)
        select = (tail_index[None, :] == (KCONV - 1 - before)[:, None]).astype(jnp.float32)
        from_tail = jnp.sum(tok_tail * select[:, :, None], axis=1)
        summed = summed + kernel[KCONV - 1 - lag_steps] * jnp.where((before > 0)[:, None], from_tail, shifted)
    return jax.nn.silu(summed + shift_bias)


def ssd_head(x_head, dt_head, rate_head, skip_head, h_head, scores, c_wide, b_wide, req_tok, starts, req_total):
    length = x_head.shape[0]
    positions = jnp.arange(length, dtype=jnp.int32)
    log_decay = -rate_head * dt_head
    cumul = jnp.cumsum(log_decay)
    cum_before = cumul - log_decay
    inside = (req_tok[:, None] == req_tok[None, :]) & (positions[:, None] >= positions[None, :])
    decay_mat = jnp.where(inside, jnp.exp(jnp.where(inside, cumul[:, None] - cumul[None, :], 0.0)), 0.0)
    mixing = (scores * decay_mat * dt_head[None, :]).astype(jnp.bfloat16)
    local_out = jnp.dot(mixing, x_head, preferred_element_type=jnp.float32)
    slot_ids = jnp.arange(REQ_GRP, dtype=jnp.int32)
    member = req_tok[None, :] == slot_ids[:, None]
    carried = jnp.einsum("tn,kpn->ktp", c_wide, h_head, precision=highest_mode)
    carry_tok = jnp.sum(jnp.where(member[:, :, None], carried, 0.0), axis=0)
    own_start = jnp.take(starts, req_tok)
    init_decay = jnp.exp(cumul - jnp.take(cum_before, own_start))
    x_wide = x_head.astype(jnp.float32)
    y_head = local_out + init_decay[:, None] * carry_tok + skip_head * x_wide
    next_start = jnp.concatenate([starts[1:], jnp.full((1,), length, jnp.int32)])
    last_index = (jnp.minimum(next_start, length) - 1).astype(jnp.int32)
    first_index = jnp.minimum(starts, length - 1).astype(jnp.int32)
    cum_end = jnp.take(cumul, last_index)
    weights = jnp.where(member, jnp.exp(jnp.where(member, cum_end[:, None] - cumul[None, :], 0.0)), 0.0) * dt_head[None, :]
    weighted = weights[:, :, None] * x_wide[None, :, :]
    gained = jnp.einsum("ktp,tn->kpn", weighted, b_wide, precision=highest_mode)
    total_decay = jnp.exp(cum_end - jnp.take(cum_before, first_index))
    new_head = total_decay[:, None, None] * h_head + gained
    return y_head, jnp.where((slot_ids < req_total)[:, None, None], new_head, 0.0)


def reference(hidden, w_x, w_small, conv_x, conv_x_bias, conv_bc, conv_bc_bias, rate, dt_bias, dskip, old_state, x_tail, bc_tail, req_count, req_source, req_start):
    heads_grp = HEADS // NGRP
    bc_width = 2 * NGRP * DSTATE

    def one_group(group_index):
        group_rows = lax.dynamic_slice_in_dim(hidden, group_index * TOK_GRP, TOK_GRP, 0)
        x_pre = jnp.dot(group_rows, w_x, preferred_element_type=jnp.float32).astype(jnp.bfloat16)
        small_proj = jnp.dot(group_rows, w_small, preferred_element_type=jnp.float32)
        sources = req_source[group_index]
        starts = req_start[group_index]
        req_total = req_count[group_index]
        h_served = jnp.take(old_state, sources, axis=0)
        x_served = jnp.take(x_tail, sources, axis=0)
        bc_served = jnp.take(bc_tail, sources, axis=0)
        req_tok = token_requests(starts, TOK_GRP)
        x_conv = causal_conv(x_pre, x_served, starts, req_tok, conv_x, conv_x_bias).astype(jnp.bfloat16)
        dt_all = jax.nn.softplus(small_proj[:, bc_width:] + dt_bias[None, :])
        y_parts = []
        state_parts = []
        for bc_group in range(NGRP):
            b_low = bc_group * DSTATE
            c_low = NGRP * DSTATE + bc_group * DSTATE
            b_conv = causal_conv(small_proj[:, b_low:b_low + DSTATE], bc_served[:, :, b_low:b_low + DSTATE], starts, req_tok, conv_bc[:, b_low:b_low + DSTATE], conv_bc_bias[b_low:b_low + DSTATE]).astype(jnp.bfloat16)
            c_conv = causal_conv(small_proj[:, c_low:c_low + DSTATE], bc_served[:, :, c_low:c_low + DSTATE], starts, req_tok, conv_bc[:, c_low:c_low + DSTATE], conv_bc_bias[c_low:c_low + DSTATE]).astype(jnp.bfloat16)
            scores = jnp.dot(c_conv, b_conv.T, preferred_element_type=jnp.float32)
            head_low = bc_group * heads_grp
            x_grp = x_conv[:, head_low * P_SIZE:(head_low + heads_grp) * P_SIZE].reshape(TOK_GRP, heads_grp, P_SIZE)
            y_grp, new_grp = jax.vmap(ssd_head, in_axes=(1, 1, 0, 0, 1, None, None, None, None, None, None), out_axes=(1, 1))(
                x_grp, dt_all[:, head_low:head_low + heads_grp], rate[head_low:head_low + heads_grp],
                dskip[head_low:head_low + heads_grp], h_served[:, head_low:head_low + heads_grp], scores,
                c_conv.astype(jnp.float32), b_conv.astype(jnp.float32), req_tok, starts, req_total)
            y_parts.append(y_grp.reshape(TOK_GRP, heads_grp * P_SIZE))
            state_parts.append(new_grp)
        return jnp.concatenate(y_parts, axis=1).astype(jnp.bfloat16), jnp.concatenate(state_parts, axis=1)

    y_all, state_all = lax.map(one_group, jnp.arange(GROUPS, dtype=jnp.int32))
    return y_all.reshape(TOKENS, HEADS * P_SIZE), state_all.reshape(SLOTS, HEADS, P_SIZE, DSTATE)
```

```python
import functools

import jax
import jax.numpy as jnp
from jax import lax
from jax.experimental import pallas as pl
from jax.experimental.pallas import tpu as pltpu
from jax.sharding import PartitionSpec as P


TOK = 512
STATES = 256
CHAN = 256
HEAD_DEV = 4
P_SIZE = 64
REQ = 4
GROUPS = 16
GROUP = ("x", "ylo", "core")
SHARD = ("yhi", "z")
PAY = 272
SMALL = 72


bf16 = jnp.bfloat16
f32 = jnp.float32
NT = (((1,), (1,)), ((), ()))
HIGH = lax.Precision.HIGHEST


def iota(shape, dim):
    return lax.broadcasted_iota(jnp.int32, shape, dim)


def call(kernel, scalars, operands, outs, flops=0, moved=0):
    smem = pl.BlockSpec(memory_space=pltpu.SMEM)
    whole = pl.BlockSpec(memory_space=pltpu.VMEM)
    return pl.pallas_call(
        kernel,
        in_specs=[smem] * len(scalars) + [whole] * len(operands),
        out_specs=jax.tree.map(lambda _: whole, outs),
        out_shape=outs,
        compiler_params=pltpu.CompilerParams(vmem_limit_bytes=48 << 20),
        cost_estimate=pl.CostEstimate(flops=flops, bytes_accessed=moved, transcendentals=0),
    )(*scalars, *operands)


def array(dtype, *shape):
    return jax.ShapeDtypeStruct(shape, dtype)


def bounds(starts_ref):
    starts = [starts_ref[k] for k in range(REQ)]
    ends = [jnp.minimum(s, TOK) for s in starts[1:]] + [jnp.int32(TOK)]
    return starts, ends


def own_start(tok, starts):
    out = jnp.zeros_like(tok)
    for k in range(1, REQ):
        out = jnp.where(tok >= starts[k], starts[k], out)
    return out


def by_request(tok, starts, values):
    out = values[0]
    for k in range(1, REQ):
        out = jnp.where(tok >= starts[k], values[k], out)
    return out


def sigmoid_gate(v):
    return v * jax.nn.sigmoid(v)


def tail_rows(tails, taps, rows, width):
    place = iota((rows, width), 0)
    out = jnp.zeros((rows, width), f32)
    for k in range(REQ):
        for d in range(3):
            term = jnp.zeros((1, width), f32)
            for j in range(d + 1, 4):
                term = term + taps[3 - j] * tails[k][3 + d - j]
            out = jnp.where(place == d * REQ + k, term, out)
    return out


def first_tokens(shape, tok_dim, starts, ends):
    tok = iota(shape, tok_dim)
    place = iota(shape, 1 - tok_dim)
    out = jnp.zeros(shape, f32)
    for k in range(REQ):
        for d in range(3):
            hit = (place == d * REQ + k) & (tok == starts[k] + d) & (tok < ends[k])
            out = jnp.where(hit, 1.0, out)
    return out


def pack_kernel(slot_ref, state_ref, tail_ref, out_ref):
    @pl.loop(0, GROUPS)
    def _(i):
        slot = slot_ref[i]
        out_ref[i, :STATES, :] = state_ref[slot].astype(bf16)
        out_ref[i, STATES:, :] = tail_ref[slot].astype(bf16)


def arrange_kernel(z_ref, own, r1, r2, r3, l1, l2, l3, far_a, far_b, hz_ref):
    def put(block, step, low, high):
        place = pl.multiple_of(lax.rem(z_ref[0] + step + 8, 8) * CHAN, CHAN)
        hz_ref[low:high, pl.ds(place, CHAN)] = block[...]

    for step, block in ((0, own), (-1, r1), (-2, r2), (-3, r3), (1, l1), (2, l2), (3, l3)):
        put(block, step, 0, TOK)
    put(far_a, 4, 0, TOK // 2)
    put(far_b, 4, TOK // 2, TOK)


def small_kernel(core_ref, hz_ref, wo_ref, wx_ref, out_ref):
    rows = hz_ref[...]
    for ref, place in ((wo_ref, core_ref[0]), (wx_ref, 1 - core_ref[0])):
        cols = jnp.concatenate([ref[s] for s in range(8)], axis=1)
        out_ref[place] = lax.dot_general(cols, rows, NT, preferred_element_type=f32)


def conv_kernel(starts_ref, src_ref, part_ref, served_ref, taps_ref, bc_ref, dt_ref):
    starts, ends = bounds(starts_ref)
    signal = part_ref[0] + part_ref[1] + part_ref[2] + part_ref[3]
    dt_ref[...] = signal[64:]
    signal = signal[:64]
    taps = [taps_ref[i : i + 1, :] for i in range(4)]
    tails = []
    for k in range(REQ):
        rows = served_ref[src_ref[k], STATES:, :].astype(f32)
        tails.append([rows[3 + i : 4 + i, :128] for i in range(3)])
    table = jnp.concatenate(
        [
            tail_rows(tails, taps, 16, 128),
            taps_ref[...],
            jnp.zeros((104, 128), f32),
        ],
        axis=0,
    ).T
    onehot = first_tokens((128, TOK), 1, starts, ends)
    corr = jnp.dot(table, onehot, precision=HIGH, preferred_element_type=f32)[:64]
    tok = iota((64, TOK), 1)
    begin = own_start(tok, starts)
    summed = table[:64, 19:20] * signal + corr + table[:64, 20:21]
    for j in range(1, 4):
        moved = jnp.where(tok - j >= begin, pltpu.roll(signal, j, 1), 0.0)
        summed = summed + table[:64, 19 - j : 20 - j] * moved
    bc_ref[...] = sigmoid_gate(summed).astype(bf16)


def product(hz_ref, w_ref):
    return jnp.dot(hz_ref[...], w_ref[...], preferred_element_type=f32)


def far_kernel(index_ref, hz_ref, w_ref, low_ref, high_ref):
    total = product(hz_ref, w_ref).astype(bf16)
    low_ref[...] = total[: TOK // 2]
    high_ref[...] = total[TOK // 2 :]


def own_kernel(index_ref, hz_ref, w_ref, out_ref):
    out_ref[...] = product(hz_ref, w_ref)


def near_kernel(low, index_ref, hz_ref, w_ref, add_ref, out_ref):
    total = product(hz_ref, w_ref)
    out_ref[...] = total.astype(bf16)
    rows = slice(low, low + TOK // 2)
    out_ref[rows, :] = (total[rows] + add_ref[...].astype(f32)).astype(bf16)


def partial(kernel, index, operands, outs):
    whole = pl.BlockSpec(memory_space=pltpu.VMEM)
    block = pl.BlockSpec((None, 8 * CHAN, CHAN), lambda i, b: (b[0], 0, 0))
    return pl.pallas_call(
        kernel,
        grid_spec=pltpu.PrefetchScalarGridSpec(
            num_scalar_prefetch=1,
            grid=(1,),
            in_specs=[whole, block] + [whole] * (len(operands) - 2),
            out_specs=jax.tree.map(lambda _: whole, outs),
        ),
        out_shape=outs,
        compiler_params=pltpu.CompilerParams(vmem_limit_bytes=48 << 20),
        cost_estimate=pl.CostEstimate(
            flops=2 * 512 * 2048 * 256, bytes_accessed=3 << 20, transcendentals=0
        ),
    )(index, *operands)


def mixing_kernel(
    starts_ref, src_ref, rate_ref, bias_ref, bc_ref, dt_ref, served_ref, par_ref,
    mix_ref, carry_ref, cols_ref, decay_ref, b_ref, tail_ref,
):
    starts, ends = bounds(starts_ref)
    taps = [par_ref[i : i + 1, :] for i in range(4)]
    tails = []
    for k in range(REQ):
        rows = served_ref[src_ref[k], STATES:, :].astype(f32)
        tails.append([rows[i : i + 1, :] for i in range(3)])
    table = tail_rows(tails, taps, 128, CHAN)
    onehot = first_tokens((TOK, 128), 0, starts, ends)
    tail_ref[...] = jnp.dot(onehot, table, precision=HIGH, preferred_element_type=f32)
    b_rows = jnp.concatenate([bc_ref[s, 0:32, :] for s in range(8)], axis=0)
    c_rows = jnp.concatenate([bc_ref[s, 32:64, :] for s in range(8)], axis=0)
    b_ref[...] = b_rows
    c_cols = c_rows.astype(f32).T.astype(bf16)
    scores = jnp.dot(c_cols, b_rows, preferred_element_type=f32)

    row = iota((8, TOK), 0)
    tok = iota((8, TOK), 1)
    rate = jnp.zeros((8, TOK), f32)
    bias = jnp.zeros((8, TOK), f32)
    for h in range(HEAD_DEV):
        rate = jnp.where(row == h, rate_ref[h], rate)
        bias = jnp.where(row == h, bias_ref[h], bias)
    raw = dt_ref[0:8, :] + bias
    dt = jnp.maximum(raw, 0.0) + jnp.log1p(jnp.exp(-jnp.abs(raw)))
    decay = -rate * dt
    cum = decay
    step = 1
    while step < TOK:
        cum = cum + jnp.where(tok >= step, pltpu.roll(cum, step, 1), 0.0)
        step *= 2
    before = cum - decay
    at_start, at_end = [], []
    for k in range(REQ):
        first = jnp.minimum(starts[k], TOK - 1)
        at_start.append(jnp.sum(jnp.where(tok == first, before, 0.0), axis=1, keepdims=True))
        at_end.append(jnp.sum(jnp.where(tok == ends[k] - 1, cum, 0.0), axis=1, keepdims=True))
        decay_ref[k] = jnp.broadcast_to(jnp.exp(at_end[k] - at_start[k]), (8, 128))
    full_start = [jnp.broadcast_to(v, (8, TOK)) for v in at_start]
    full_end = [jnp.broadcast_to(v, (8, TOK)) for v in at_end]
    carried_decay = jnp.exp(cum - by_request(tok, starts, full_start))
    weight = jnp.exp(by_request(tok, starts, full_end) - cum) * dt
    cols = jnp.concatenate([cum, carried_decay, weight, jnp.zeros((104, TOK), f32)], axis=0).T
    cols_ref[...] = cols

    tok_c = iota((TOK, CHAN), 0)
    lane = iota((TOK, CHAN), 1)
    carry = jnp.zeros((TOK, CHAN), f32)
    for k in range(REQ):
        old = served_ref[src_ref[k], :CHAN, :]
        part = lax.dot_general(c_cols, old, NT, preferred_element_type=f32)
        carry = jnp.where((tok_c >= starts[k]) & (tok_c < ends[k]), part, carry)
    scale = jnp.zeros((TOK, CHAN), f32)
    for h in range(HEAD_DEV):
        scale = jnp.where(lane >= h * P_SIZE, cols[:, 8 + h : 9 + h], scale)
    carry_ref[...] = carry * scale

    for b in range(4):
        low, width = b * 128, (b + 1) * 128
        tok_t = iota((128, width), 0) + low
        tok_s = iota((128, width), 1)
        inside = (tok_s <= tok_t) & (tok_s >= own_start(tok_t, starts))
        block = scores[low : low + 128, :width]
        for h in range(HEAD_DEV):
            gap = cols[low : low + 128, h : h + 1] - cum[h : h + 1, :width]
            grown = jnp.exp(jnp.where(inside, gap, 0.0))
            value = jnp.where(inside, block * grown * dt[h : h + 1, :width], 0.0)
            mix_ref[h, low : low + 128, 0:width] = value.astype(bf16)


def output_kernel(
    starts_ref, src_ref, count_ref, x0, x1, x2, served_ref, par_ref,
    mix_ref, carry_ref, cols_ref, decay_ref, b_ref, tail_ref, y_ref, state_ref,
):
    starts, ends = bounds(starts_ref)
    count = count_ref[0]
    signal = x0[...] + x1[...].astype(f32) + x2[...].astype(f32)
    taps = [par_ref[i : i + 1, :] for i in range(4)]
    summed = tail_ref[...]
    tok = iota((TOK, CHAN), 0)
    lane = iota((TOK, CHAN), 1)
    begin = own_start(tok, starts)
    summed = summed + taps[3] * signal + par_ref[4:5, :]
    for j in range(1, 4):
        moved = jnp.where(tok - j >= begin, pltpu.roll(signal, j, 0), 0.0)
        summed = summed + taps[3 - j] * moved
    x_low = sigmoid_gate(summed).astype(bf16)
    x_wide = x_low.astype(f32)
    base = carry_ref[...] + par_ref[5:6, :] * x_wide
    for b in range(4):
        low, width = b * 128, (b + 1) * 128
        total = base[low : low + 128]
        for h in range(HEAD_DEV):
            mine = (lane[:width] >= h * P_SIZE) & (lane[:width] < (h + 1) * P_SIZE)
            x_head = jnp.where(mine, x_wide[:width], 0.0).astype(bf16)
            total = total + jnp.dot(
                mix_ref[h, low : low + 128, 0:width], x_head, preferred_element_type=f32
            )
        y_ref[low : low + 128, :] = total.astype(bf16)

    weight = jnp.zeros((TOK, CHAN), f32)
    for h in range(HEAD_DEV):
        weight = jnp.where(lane >= h * P_SIZE, cols_ref[:, 16 + h : 17 + h], weight)
    weighted = (x_wide * weight).T
    high = weighted.astype(bf16).astype(f32)
    rest = weighted - high
    tok_r = iota((CHAN, TOK), 1)
    b_rows = b_ref[...]
    for k in range(REQ):
        member = (tok_r >= starts[k]) & (tok_r < ends[k])
        gained = lax.dot_general(
            jnp.where(member, high, 0.0).astype(bf16), b_rows, NT, preferred_element_type=f32
        ) + lax.dot_general(
            jnp.where(member, rest, 0.0).astype(bf16), b_rows, NT, preferred_element_type=f32
        )
        for h in range(HEAD_DEV):
            lo, hi = h * P_SIZE, (h + 1) * P_SIZE
            old = served_ref[src_ref[k], lo:hi, :].astype(f32)
            new = decay_ref[k, h : h + 1, 0:1] * old + gained[lo:hi]
            state_ref[k, lo:hi, :] = jnp.where(k < count, new, 0.0)


def layer(
    hidden, w_x, w_small, conv_x, conv_x_bias, conv_bc, conv_bc_bias, rate, dt_bias, dskip,
    old_state, x_tail, bc_tail, req_count, req_source, req_start,
):
    group = lax.axis_index(GROUP)
    core = lax.axis_index("core")
    yhi = lax.axis_index("yhi")
    z = lax.axis_index("z")
    mine = lax.dynamic_index_in_dim(req_source, group, 0, keepdims=False)
    src = mine // REQ
    starts = lax.dynamic_index_in_dim(req_start, group, 0, keepdims=False)
    count = lax.dynamic_slice_in_dim(req_count, group, 1, 0)

    swap = [(a * 4 + b, b * 4 + a) for a in range(4) for b in range(4)]
    w_swapped = lax.ppermute(w_x, ("x", "yhi"), swap)
    w_all = lax.all_gather(w_swapped, GROUP, axis=0, tiled=False)

    up = [(i, (i + 1) % 8) for i in range(8)]
    down = [(i, (i - 1) % 8) for i in range(8)]
    blocks = [hidden]
    for ring in (up, down):
        block = hidden
        for _ in range(3):
            block = lax.ppermute(block, "z", ring)
            blocks.append(block)
    half = TOK // 2
    blocks.append(lax.ppermute(blocks[3][:half], "z", up))
    blocks.append(lax.ppermute(blocks[6][half:], "z", down))

    w_t = w_small.T
    w_b = w_t[:1024].reshape(4, 8, 32, 256)
    w_c = w_t[1024:2048].reshape(4, 8, 32, 256)
    w_d = jnp.pad(w_t[2048:].reshape(4, 8, 4, 256), ((0, 0), (0, 0), (0, SMALL - 68), (0, 0)))
    w_cols = jnp.concatenate([w_b, w_c, w_d], axis=2)
    w_cols = lax.dynamic_slice_in_dim(w_cols, core * 2, 2, 0)
    w_cols = w_cols.transpose(1, 0, 2, 3).reshape(8, 2 * SMALL, 256)
    w_cols = lax.all_to_all(w_cols, "z", 0, 0, tiled=True)
    w_other = lax.ppermute(w_cols, "core", [(0, 1), (1, 0)])

    owner, slot = req_source // REQ, req_source % REQ
    slots = jnp.sum(jnp.where(owner == group, slot, 0), axis=1).astype(jnp.int32)
    bc_mine = lax.dynamic_slice(
        bc_tail.reshape(REQ, 3, 2, 4, 8, 32), (0, 0, 0, yhi, z, 0), (REQ, 3, 2, 1, 1, 32)
    ).reshape(REQ, 3, 64)
    tails = jnp.concatenate(
        [x_tail, jnp.pad(bc_mine, ((0, 0), (0, 0), (0, 192))), jnp.zeros((REQ, 10, 256), f32)],
        axis=1,
    )
    packed = call(
        pack_kernel,
        (slots,),
        (old_state.reshape(REQ, 256, STATES), tails),
        array(bf16, GROUPS, PAY, 256),
        moved=7 << 20,
    )
    served = lax.all_to_all(packed, GROUP, 0, 0, tiled=True)

    hz = call(
        arrange_kernel,
        (z.astype(jnp.int32).reshape(1),),
        blocks,
        array(bf16, TOK, 8 * CHAN),
        moved=4 << 20,
    )
    part_small = call(
        small_kernel,
        (core.astype(jnp.int32).reshape(1),),
        (hz, w_cols, w_other),
        array(f32, 2, 2 * SMALL, TOK),
        flops=2 * 288 * 2048 * 512,
        moved=4 << 20,
    )
    part_small = lax.all_to_all(part_small.reshape(4, SMALL, TOK), "yhi", 0, 0, tiled=True)

    taps_bc = lax.dynamic_slice(
        conv_bc.reshape(4, 2, 4, 8, 32), (0, 0, yhi, z, 0), (4, 2, 1, 1, 32)
    ).reshape(4, 64)
    bias_bc = lax.dynamic_slice(
        conv_bc_bias.reshape(2, 4, 8, 32), (0, yhi, z, 0), (2, 1, 1, 32)
    ).reshape(1, 64)
    taps_bc = jnp.pad(jnp.concatenate([taps_bc, bias_bc], axis=0), ((0, 3), (0, 64)))
    bc_own, dt_raw = call(
        conv_kernel,
        (starts, src),
        (part_small, served, taps_bc),
        (array(bf16, 64, TOK), array(f32, SMALL - 64, TOK)),
        flops=2 * 6 * 128 * 128 * 512,
        moved=1 << 20,
    )
    bc_all = lax.all_to_all(
        jnp.broadcast_to(bc_own[None], (8, 64, TOK)), "z", 0, 0, tiled=True
    )

    w_view = w_all.reshape(4, 8 * CHAN, CHAN)
    index = [((yhi + r) % 4).astype(jnp.int32).reshape(1) for r in range(4)]
    ahead = [(i, (i + 1) % 4) for i in range(4)]
    back = [(i, (i - 1) % 4) for i in range(4)]
    low, high = partial(far_kernel, index[2], (hz, w_view), (array(bf16, half, CHAN),) * 2)
    low = lax.ppermute(low, "yhi", ahead)
    high = lax.ppermute(high, "yhi", back)
    x0 = partial(own_kernel, index[0], (hz, w_view), array(f32, TOK, CHAN))
    x1 = partial(
        functools.partial(near_kernel, 0),
        index[1], (hz, w_view, low), array(bf16, TOK, CHAN),
    )
    x1 = lax.ppermute(x1, "yhi", ahead)
    x2 = partial(
        functools.partial(near_kernel, half),
        index[3], (hz, w_view, high), array(bf16, TOK, CHAN),
    )
    x2 = lax.ppermute(x2, "yhi", back)

    params = jnp.concatenate(
        [conv_x, conv_x_bias[None], jnp.repeat(dskip, P_SIZE)[None], jnp.zeros((2, CHAN), f32)],
        axis=0,
    )
    made = call(
        mixing_kernel,
        (starts, src, rate, dt_bias),
        (bc_all, dt_raw, served, params),
        (
            array(bf16, HEAD_DEV, TOK, TOK),
            array(f32, TOK, CHAN),
            array(f32, TOK, 128),
            array(f32, REQ, 8, 128),
            array(bf16, STATES, TOK),
            array(f32, TOK, CHAN),
        ),
        flops=2 * 8 * 512 * 256 * 256,
        moved=12 << 20,
    )
    y, state = call(
        output_kernel,
        (starts, src, count),
        (x0, x1, x2, served, params, *made),
        (array(bf16, TOK, CHAN), array(f32, REQ, 256, STATES)),
        flops=2 * 20 * 512 * 256 * 256,
        moved=6 << 20,
    )
    return y, state.reshape(REQ, HEAD_DEV, P_SIZE, STATES)


def solution(mesh):
    fine = jax.sharding.Mesh(mesh.devices.reshape(4, 2, 2, 4, 8), ("x", "ylo", "core", "yhi", "z"))
    g, s = GROUP, SHARD
    in_specs = (
        P(g, s),
        P(g, s),
        P(s, None),
        P(None, s),
        P(s),
        P(),
        P(),
        P(s),
        P(s),
        P(s),
        P(g, s, None, None),
        P(g, None, s),
        P(g, None, None),
        P(),
        P(),
        P(),
    )
    out_specs = (P(g, s), P(g, s, None, None))
    return jax.shard_map(layer, mesh=fine, in_specs=in_specs, out_specs=out_specs, check_vma=False)
```

```python
import functools

import jax
import jax.numpy as jnp
from jax import lax
from jax.experimental import pallas as pl
from jax.experimental.pallas import tpu as pltpu
from jax.sharding import PartitionSpec as P


TOK = 512
STATES = 256
CHAN = 256
HEAD_DEV = 4
P_SIZE = 64
REQ = 4
GROUPS = 16
GROUP = ("x", "ylo", "core")
SHARD = ("yhi", "z")
SMALL = 72
PAY = 272


bf16 = jnp.bfloat16
f32 = jnp.float32
NT = (((1,), (1,)), ((), ()))
HIGH = lax.Precision.HIGHEST


def iota(shape, dim):
    return lax.broadcasted_iota(jnp.int32, shape, dim)


def call(kernel, scalars, operands, outs, flops=0, moved=0, scratch=(), room=8):
    smem = pl.BlockSpec(memory_space=pltpu.SMEM)
    whole = pl.BlockSpec(memory_space=pltpu.VMEM)
    return pl.pallas_call(
        kernel,
        in_specs=[smem] * len(scalars) + [whole] * len(operands),
        out_specs=jax.tree.map(lambda _: whole, outs),
        out_shape=outs,
        scratch_shapes=scratch,
        compiler_params=pltpu.CompilerParams(vmem_limit_bytes=room << 20),
        cost_estimate=pl.CostEstimate(flops=flops, bytes_accessed=moved, transcendentals=0),
    )(*scalars, *operands)


def array(dtype, *shape):
    return jax.ShapeDtypeStruct(shape, dtype)


def group_index():
    return lax.axis_index("x") * 4 + lax.axis_index("ylo") * 2 + lax.axis_index("core")


def bounds(starts_ref):
    group = group_index()
    starts = [starts_ref[k, group] for k in range(REQ)]
    ends = [jnp.minimum(s, TOK) for s in starts[1:]] + [jnp.int32(TOK)]
    return starts, ends


def owners(src_ref):
    group = group_index()
    return [src_ref[k, group] >> 2 for k in range(REQ)]


def bc_lanes(read):
    yhi, z = lax.axis_index("yhi"), lax.axis_index("z")
    block, offset = yhi * 2 + (z >> 2), (z & 3) * 32
    b = pltpu.roll(read(block), (128 - offset) & 127, 1)
    c = pltpu.roll(read(block + 8), (160 - offset) & 127, 1)
    lane = iota(b.shape, 1)
    return jnp.where(lane < 32, b, jnp.where(lane < 64, c, 0.0))


def own_start(tok, starts):
    out = jnp.zeros_like(tok)
    for k in range(1, REQ):
        out = jnp.where(tok >= starts[k], starts[k], out)
    return out


def by_request(tok, starts, values):
    out = values[0]
    for k in range(1, REQ):
        out = jnp.where(tok >= starts[k], values[k], out)
    return out


def sigmoid_gate(v):
    return v * jax.nn.sigmoid(v)


def tail_rows(tails, taps, rows, width):
    place = iota((rows, width), 0)
    out = jnp.zeros((rows, width), f32)
    for k in range(REQ):
        for d in range(3):
            term = jnp.zeros((1, width), f32)
            for j in range(d + 1, 4):
                term = term + taps[3 - j] * tails[k][3 + d - j]
            out = jnp.where(place == d * REQ + k, term, out)
    return out


def first_tokens(shape, tok_dim, starts, ends):
    tok = iota(shape, tok_dim)
    place = iota(shape, 1 - tok_dim)
    out = jnp.zeros(shape, f32)
    for k in range(REQ):
        for d in range(3):
            hit = (place == d * REQ + k) & (tok == starts[k] + d) & (tok < ends[k])
            out = jnp.where(hit, 1.0, out)
    return out


def slot_for(src_ref, target):
    group = group_index()
    slot = jnp.int32(0)
    for k in range(REQ):
        place = src_ref[k, target]
        slot = jnp.where((place >> 2) == group, place & 3, slot)
    return slot


def pack_kernel(src_ref, state_ref, x_ref, bc_ref, out_ref, tmp_ref):
    row = iota((16, CHAN), 0)
    wide = [
        bc_lanes(lambda block, i=i: bc_ref[i, :, pl.ds(pl.multiple_of(block * 128, 128), 128)])
        for i in range(3)
    ]
    for slot in range(REQ):
        value = jnp.zeros((16, CHAN), f32)
        for i in range(3):
            value = jnp.where(row == i, x_ref[i, slot : slot + 1, :], value)
            line = jnp.concatenate([wide[i][slot : slot + 1], jnp.zeros((1, 128), f32)], axis=1)
            value = jnp.where(row == 3 + i, line, value)
        tmp_ref[slot] = value.astype(bf16)

    @pl.loop(0, GROUPS)
    def _(i):
        slot = slot_for(src_ref, i)
        out_ref[i, :STATES, :] = state_ref[slot].astype(bf16)
        out_ref[i, STATES:, :] = tmp_ref[slot]


def place_kernel(plan, count, *refs):
    blocks, hz_ref, sems = refs[:count], refs[-2], refs[-1]
    copies = []
    for i, (step, low) in enumerate(plan):
        block = blocks[count - len(plan) + i]
        place = pl.multiple_of(((lax.axis_index("z") + step + 8) & 7) * CHAN, CHAN)
        target = hz_ref.at[low : low + block.shape[0], pl.ds(place, CHAN)]
        copies.append(pltpu.make_async_copy(block, target, sems.at[i]))
        copies[-1].start()
    for copy in copies:
        copy.wait()


def place_blocks(plan, operands):
    anywhere = pl.BlockSpec(memory_space=pl.ANY)
    return pl.pallas_call(
        functools.partial(place_kernel, plan, len(operands)),
        in_specs=[anywhere] * len(operands),
        out_specs=anywhere,
        out_shape=array(bf16, TOK, 8 * CHAN),
        input_output_aliases={0: 0} if len(operands) > len(plan) else {},
        scratch_shapes=[pltpu.SemaphoreType.DMA((len(plan),))],
        compiler_params=pltpu.CompilerParams(vmem_limit_bytes=4 << 20),
        cost_estimate=pl.CostEstimate(flops=0, bytes_accessed=1 << 20, transcendentals=0),
        name="place_blocks",
    )(*operands)


def small_kernel(hz_ref, wo_ref, wx_ref, out_ref):
    rows = hz_ref[...]
    core = lax.axis_index("core")
    for ref, place in ((wo_ref, core), (wx_ref, 1 - core)):
        cols = jnp.concatenate([ref[s] for s in range(8)], axis=1)
        out_ref[place] = lax.dot_general(cols, rows, NT, preferred_element_type=f32)


def conv_kernel(starts_ref, src_ref, part_ref, served_ref, taps_ref, bias_ref, bc_ref, dt_ref):
    starts, ends = bounds(starts_ref)
    src = owners(src_ref)
    signal = part_ref[0] + part_ref[1] + part_ref[2] + part_ref[3]
    dt_ref[...] = signal[64:]
    signal = signal[:64]
    own_taps = bc_lanes(lambda block: taps_ref[:, pl.ds(pl.multiple_of(block * 128, 128), 128)])
    own_bias = bc_lanes(lambda block: bias_ref[pl.ds(block, 1), :])
    taps = [own_taps[i : i + 1] for i in range(4)]
    tails = []
    for k in range(REQ):
        rows = served_ref[src[k], STATES:, :].astype(f32)
        tails.append([rows[3 + i : 4 + i, :128] for i in range(3)])
    table = jnp.concatenate(
        [
            tail_rows(tails, taps, 16, 128),
            own_taps,
            own_bias,
            jnp.zeros((107, 128), f32),
        ],
        axis=0,
    ).T
    onehot = first_tokens((128, TOK), 1, starts, ends)
    corr = jnp.dot(table, onehot, precision=HIGH, preferred_element_type=f32)[:64]
    tok = iota((64, TOK), 1)
    begin = own_start(tok, starts)
    summed = table[:64, 19:20] * signal + corr + table[:64, 20:21]
    for j in range(1, 4):
        moved = jnp.where(tok - j >= begin, pltpu.roll(signal, j, 1), 0.0)
        summed = summed + table[:64, 19 - j : 20 - j] * moved
    bc_ref[...] = sigmoid_gate(summed).astype(bf16)


def product(hz_ref, w_ref):
    return jnp.dot(hz_ref[...], w_ref[...], preferred_element_type=f32)


def far_kernel(index_ref, hz_ref, w_ref, low_ref, high_ref):
    total = product(hz_ref, w_ref).astype(bf16)
    low_ref[...] = total[: TOK // 2]
    high_ref[...] = total[TOK // 2 :]


def own_kernel(index_ref, hz_ref, w_ref, out_ref):
    out_ref[...] = product(hz_ref, w_ref)


def near_kernel(low, index_ref, hz_ref, w_ref, add_ref, out_ref):
    total = product(hz_ref, w_ref)
    out_ref[...] = total.astype(bf16)
    rows = slice(low, low + TOK // 2)
    out_ref[rows, :] = (total[rows] + add_ref[...].astype(f32)).astype(bf16)


def partial(kernel, way, operands, outs):
    whole = pl.BlockSpec(memory_space=pltpu.VMEM)
    block = pl.BlockSpec((None, 8 * CHAN, CHAN), lambda i, b: ((b[0] + way) & 3, 0, 0))
    index = lax.axis_index("yhi").astype(jnp.int32).reshape(1)
    return pl.pallas_call(
        kernel,
        grid_spec=pltpu.PrefetchScalarGridSpec(
            num_scalar_prefetch=1,
            grid=(1,),
            in_specs=[whole, block] + [whole] * (len(operands) - 2),
            out_specs=jax.tree.map(lambda _: whole, outs),
        ),
        out_shape=outs,
        compiler_params=pltpu.CompilerParams(vmem_limit_bytes=48 << 20),
        cost_estimate=pl.CostEstimate(
            flops=2 * 512 * 2048 * 256, bytes_accessed=3 << 20, transcendentals=0
        ),
    )(index, *operands)


def mixing_kernel(
    starts_ref, src_ref, rate_ref, bias_ref, bc_ref, dt_ref, served_ref, taps_ref,
    mix_ref, carry_ref, cols_ref, decay_ref, b_ref, tail_ref,
):
    starts, ends = bounds(starts_ref)
    src = owners(src_ref)
    taps = [taps_ref[i : i + 1, :] for i in range(4)]
    tails = []
    for k in range(REQ):
        rows = served_ref[src[k], STATES:, :].astype(f32)
        tails.append([rows[i : i + 1, :] for i in range(3)])
    table = tail_rows(tails, taps, 128, CHAN)
    onehot = first_tokens((TOK, 128), 0, starts, ends)
    tail_ref[...] = jnp.dot(onehot, table, precision=HIGH, preferred_element_type=f32)
    b_rows = jnp.concatenate([bc_ref[s, 0:32, :] for s in range(8)], axis=0)
    c_rows = jnp.concatenate([bc_ref[s, 32:64, :] for s in range(8)], axis=0)
    b_ref[...] = b_rows
    c_cols = c_rows.astype(f32).T.astype(bf16)
    scores = jnp.dot(c_cols, b_rows, preferred_element_type=f32)

    row = iota((8, TOK), 0)
    tok = iota((8, TOK), 1)
    rate = jnp.zeros((8, TOK), f32)
    bias = jnp.zeros((8, TOK), f32)
    for h in range(HEAD_DEV):
        rate = jnp.where(row == h, rate_ref[h], rate)
        bias = jnp.where(row == h, bias_ref[h], bias)
    raw = dt_ref[0:8, :] + bias
    dt = jnp.maximum(raw, 0.0) + jnp.log1p(jnp.exp(-jnp.abs(raw)))
    decay = -rate * dt
    cum = decay
    step = 1
    while step < TOK:
        cum = cum + jnp.where(tok >= step, pltpu.roll(cum, step, 1), 0.0)
        step *= 2
    before = cum - decay
    at_start, at_end = [], []
    for k in range(REQ):
        first = jnp.minimum(starts[k], TOK - 1)
        at_start.append(jnp.sum(jnp.where(tok == first, before, 0.0), axis=1, keepdims=True))
        at_end.append(jnp.sum(jnp.where(tok == ends[k] - 1, cum, 0.0), axis=1, keepdims=True))
        decay_ref[k] = jnp.broadcast_to(jnp.exp(at_end[k] - at_start[k]), (8, 128))
    full_start = [jnp.broadcast_to(v, (8, TOK)) for v in at_start]
    full_end = [jnp.broadcast_to(v, (8, TOK)) for v in at_end]
    carried_decay = jnp.exp(cum - by_request(tok, starts, full_start))
    weight = jnp.exp(by_request(tok, starts, full_end) - cum) * dt
    cols = jnp.concatenate([cum, carried_decay, weight, jnp.zeros((104, TOK), f32)], axis=0).T
    cols_ref[...] = cols

    tok_c = iota((TOK, CHAN), 0)
    lane = iota((TOK, CHAN), 1)
    carry = jnp.zeros((TOK, CHAN), f32)
    for k in range(REQ):
        old = served_ref[src[k], :CHAN, :]
        part = lax.dot_general(c_cols, old, NT, preferred_element_type=f32)
        carry = jnp.where((tok_c >= starts[k]) & (tok_c < ends[k]), part, carry)
    scale = jnp.zeros((TOK, CHAN), f32)
    for h in range(HEAD_DEV):
        scale = jnp.where(lane >= h * P_SIZE, cols[:, 8 + h : 9 + h], scale)
    carry_ref[...] = carry * scale

    for b in range(4):
        low, width = b * 128, (b + 1) * 128
        tok_t = iota((128, width), 0) + low
        tok_s = iota((128, width), 1)
        inside = (tok_s <= tok_t) & (tok_s >= own_start(tok_t, starts))
        block = scores[low : low + 128, :width]
        for h in range(HEAD_DEV):
            gap = cols[low : low + 128, h : h + 1] - cum[h : h + 1, :width]
            grown = jnp.exp(jnp.where(inside, gap, 0.0))
            value = jnp.where(inside, block * grown * dt[h : h + 1, :width], 0.0)
            mix_ref[h, low : low + 128, 0:width] = value.astype(bf16)


def output_kernel(
    starts_ref, src_ref, count_ref, skip_ref, x0, x1, x2, served_ref, taps_ref, bias_ref,
    mix_ref, carry_ref, cols_ref, decay_ref, b_ref, tail_ref, y_ref, state_ref,
):
    starts, ends = bounds(starts_ref)
    src = owners(src_ref)
    count = count_ref[group_index()]
    signal = x0[...] + x1[...].astype(f32) + x2[...].astype(f32)
    taps = [taps_ref[i : i + 1, :] for i in range(4)]
    bias = jnp.concatenate([bias_ref[0:1, :], bias_ref[1:2, :]], axis=1)
    summed = tail_ref[...]
    tok = iota((TOK, CHAN), 0)
    lane = iota((TOK, CHAN), 1)
    begin = own_start(tok, starts)
    summed = summed + taps[3] * signal + bias
    for j in range(1, 4):
        moved = jnp.where(tok - j >= begin, pltpu.roll(signal, j, 0), 0.0)
        summed = summed + taps[3 - j] * moved
    x_low = sigmoid_gate(summed).astype(bf16)
    x_wide = x_low.astype(f32)
    skip = jnp.zeros((TOK, CHAN), f32)
    for h in range(HEAD_DEV):
        skip = jnp.where(lane >= h * P_SIZE, skip_ref[h], skip)
    base = carry_ref[...] + skip * x_wide
    for b in range(4):
        low, width = b * 128, (b + 1) * 128
        total = base[low : low + 128]
        for h in range(HEAD_DEV):
            mine = (lane[:width] >= h * P_SIZE) & (lane[:width] < (h + 1) * P_SIZE)
            x_head = jnp.where(mine, x_wide[:width], 0.0).astype(bf16)
            total = total + jnp.dot(
                mix_ref[h, low : low + 128, 0:width], x_head, preferred_element_type=f32
            )
        y_ref[low : low + 128, :] = total.astype(bf16)

    weight = jnp.zeros((TOK, CHAN), f32)
    for h in range(HEAD_DEV):
        weight = jnp.where(lane >= h * P_SIZE, cols_ref[:, 16 + h : 17 + h], weight)
    weighted = (x_wide * weight).T
    high = weighted.astype(bf16).astype(f32)
    rest = weighted - high
    tok_r = iota((CHAN, TOK), 1)
    b_rows = b_ref[...]
    for k in range(REQ):
        member = (tok_r >= starts[k]) & (tok_r < ends[k])
        gained = lax.dot_general(
            jnp.where(member, high, 0.0).astype(bf16), b_rows, NT, preferred_element_type=f32
        ) + lax.dot_general(
            jnp.where(member, rest, 0.0).astype(bf16), b_rows, NT, preferred_element_type=f32
        )
        for h in range(HEAD_DEV):
            lo, hi = h * P_SIZE, (h + 1) * P_SIZE
            old = served_ref[src[k], lo:hi, :].astype(f32)
            new = decay_ref[k, h : h + 1, 0:1] * old + gained[lo:hi]
            state_ref[k, lo:hi, :] = jnp.where(k < count, new, 0.0)


def layer(
    hidden, w_x, w_small, conv_x, conv_x_bias, conv_bc, conv_bc_bias, rate, dt_bias, dskip,
    old_state, x_tail, bc_tail, req_count, req_source, req_start,
):
    core = lax.axis_index("core")
    src, starts = req_source.T, req_start.T

    swap = [(a * 4 + b, b * 4 + a) for a in range(4) for b in range(4)]
    w_swapped = lax.ppermute(w_x, ("x", "yhi"), swap)
    w_all = lax.all_gather(w_swapped, GROUP, axis=0, tiled=False)

    up = [(i, (i + 1) % 8) for i in range(8)]
    down = [(i, (i - 1) % 8) for i in range(8)]
    blocks = [hidden]
    for ring in (up, down):
        block = hidden
        for _ in range(3):
            block = lax.ppermute(block, "z", ring)
            blocks.append(block)
    half = TOK // 2
    blocks.append(lax.ppermute(blocks[3][:half], "z", up))
    blocks.append(lax.ppermute(blocks[6][half:], "z", down))

    w_t = w_small.T
    w_b = w_t[:1024].reshape(4, 8, 32, 256)
    w_c = w_t[1024:2048].reshape(4, 8, 32, 256)
    w_d = jnp.pad(w_t[2048:].reshape(4, 8, 4, 256), ((0, 0), (0, 0), (0, SMALL - 68), (0, 0)))
    w_cols = jnp.concatenate([w_b, w_c, w_d], axis=2)
    w_cols = lax.dynamic_slice_in_dim(w_cols, core * 2, 2, 0)
    w_cols = w_cols.transpose(1, 0, 2, 3).reshape(8, 2 * SMALL, 256)
    w_cols = lax.all_to_all(w_cols, "z", 0, 0, tiled=True)
    w_other = lax.ppermute(w_cols, "core", [(0, 1), (1, 0)])

    served = call(
        pack_kernel,
        (src,),
        (
            old_state.reshape(REQ, CHAN, STATES),
            x_tail.transpose(1, 0, 2),
            bc_tail.transpose(1, 0, 2),
        ),
        array(bf16, GROUPS, PAY, STATES),
        moved=7 << 20,
        scratch=[pltpu.VMEM((REQ, 16, CHAN), bf16)],
    )
    served = lax.all_to_all(served, GROUP, 0, 0, tiled=True)

    hz = place_blocks(((0, 0), (-1, 0), (1, 0)), (hidden, blocks[1], blocks[4]))
    for step in (2, 3):
        hz = place_blocks(((-step, 0), (step, 0)), (hz, blocks[step], blocks[step + 3]))
    hz = place_blocks(((4, 0), (4, half)), (hz, blocks[7], blocks[8]))
    part_small = call(
        small_kernel,
        (),
        (hz, w_cols, w_other),
        array(f32, 2, 2 * SMALL, TOK),
        flops=2 * 288 * 2048 * 512,
        moved=4 << 20,
    )
    part_small = lax.all_to_all(part_small.reshape(4, SMALL, TOK), "yhi", 0, 0, tiled=True)

    bc_own, dt_raw = call(
        conv_kernel,
        (starts, src),
        (part_small, served, conv_bc, conv_bc_bias.reshape(16, 128)),
        (array(bf16, 64, TOK), array(f32, SMALL - 64, TOK)),
        flops=2 * 6 * 128 * 128 * 512,
        moved=1 << 20,
    )
    bc_all = lax.all_to_all(
        jnp.broadcast_to(bc_own[None], (8, 64, TOK)), "z", 0, 0, tiled=True
    )

    w_view = w_all.reshape(4, 8 * CHAN, CHAN)
    ahead = [(i, (i + 1) % 4) for i in range(4)]
    back = [(i, (i - 1) % 4) for i in range(4)]
    low, high = partial(far_kernel, 2, (hz, w_view), (array(bf16, half, CHAN),) * 2)
    low = lax.ppermute(low, "yhi", ahead)
    high = lax.ppermute(high, "yhi", back)
    x0 = partial(own_kernel, 0, (hz, w_view), array(f32, TOK, CHAN))
    x1 = partial(
        functools.partial(near_kernel, 0),
        1, (hz, w_view, low), array(bf16, TOK, CHAN),
    )
    x1 = lax.ppermute(x1, "yhi", ahead)
    x2 = partial(
        functools.partial(near_kernel, half),
        3, (hz, w_view, high), array(bf16, TOK, CHAN),
    )
    x2 = lax.ppermute(x2, "yhi", back)

    made = call(
        mixing_kernel,
        (starts, src, rate, dt_bias),
        (bc_all, dt_raw, served, conv_x),
        (
            array(bf16, HEAD_DEV, TOK, TOK),
            array(f32, TOK, CHAN),
            array(f32, TOK, 128),
            array(f32, REQ, 8, 128),
            array(bf16, STATES, TOK),
            array(f32, TOK, CHAN),
        ),
        flops=2 * 8 * 512 * 256 * 256,
        moved=12 << 20,
        room=24,
    )
    y, state = call(
        output_kernel,
        (starts, src, req_count, dskip),
        (x0, x1, x2, served, conv_x, conv_x_bias.reshape(2, 128), *made),
        (array(bf16, TOK, CHAN), array(f32, REQ, 256, STATES)),
        flops=2 * 20 * 512 * 256 * 256,
        moved=6 << 20,
        room=24,
    )
    return y, state.reshape(REQ, HEAD_DEV, P_SIZE, STATES)


def solution(mesh):
    fine = jax.sharding.Mesh(mesh.devices.reshape(4, 2, 2, 4, 8), ("x", "ylo", "core", "yhi", "z"))
    g, s = GROUP, SHARD
    in_specs = (
        P(g, s),
        P(g, s),
        P(s, None),
        P(None, s),
        P(s),
        P(),
        P(),
        P(s),
        P(s),
        P(s),
        P(g, s, None, None),
        P(g, None, s),
        P(g, None, None),
        P(),
        P(),
        P(),
    )
    out_specs = (P(g, s), P(g, s, None, None))
    return jax.shard_map(layer, mesh=fine, in_specs=in_specs, out_specs=out_specs, check_vma=False)
```

```python
import functools

import jax
import jax.numpy as jnp
from jax import lax
from jax.experimental import pallas as pl
from jax.experimental.pallas import tpu as pltpu
from jax.sharding import PartitionSpec as P


TOK = 512
STATES = 256
CHAN = 256
HEAD_DEV = 4
P_SIZE = 64
REQ = 4
GROUP = ("x", "ylo", "core")
SHARD = ("yhi", "z")
SMALL = 72
BLOCK = 576


bf16 = jnp.bfloat16
f32 = jnp.float32
NT = (((1,), (1,)), ((), ()))
HIGH = lax.Precision.HIGHEST


def iota(shape, dim):
    return lax.broadcasted_iota(jnp.int32, shape, dim)


def call(kernel, scalars, operands, outs, flops=0, moved=0, scratch=(), room=8):
    smem = pl.BlockSpec(memory_space=pltpu.SMEM)
    whole = pl.BlockSpec(memory_space=pltpu.VMEM)
    return pl.pallas_call(
        kernel,
        in_specs=[smem] * len(scalars) + [whole] * len(operands),
        out_specs=jax.tree.map(lambda _: whole, outs),
        out_shape=outs,
        scratch_shapes=scratch,
        compiler_params=pltpu.CompilerParams(vmem_limit_bytes=room << 20),
        cost_estimate=pl.CostEstimate(flops=flops, bytes_accessed=moved, transcendentals=0),
    )(*scalars, *operands)


def array(dtype, *shape):
    return jax.ShapeDtypeStruct(shape, dtype)


def group_index():
    return lax.axis_index("x") * 4 + lax.axis_index("ylo") * 2 + lax.axis_index("core")


def bounds(starts_ref):
    group = group_index()
    starts = [starts_ref[k, group] for k in range(REQ)]
    ends = [jnp.minimum(s, TOK) for s in starts[1:]] + [jnp.int32(TOK)]
    return starts, ends


def bc_lanes(read):
    yhi, z = lax.axis_index("yhi"), lax.axis_index("z")
    block, offset = yhi * 2 + (z >> 2), (z & 3) * 32
    b = pltpu.roll(read(block), (128 - offset) & 127, 1)
    c = pltpu.roll(read(block + 8), (160 - offset) & 127, 1)
    lane = iota(b.shape, 1)
    return jnp.where(lane < 32, b, jnp.where(lane < 64, c, 0.0))


def own_start(tok, starts):
    out = jnp.zeros_like(tok)
    for k in range(1, REQ):
        out = jnp.where(tok >= starts[k], starts[k], out)
    return out


def by_request(tok, starts, values):
    out = values[0]
    for k in range(1, REQ):
        out = jnp.where(tok >= starts[k], values[k], out)
    return out


def sigmoid_gate(v):
    return v * jax.nn.sigmoid(v)


def tail_rows(tails, taps, rows, width):
    place = iota((rows, width), 0)
    out = jnp.zeros((rows, width), f32)
    for k in range(REQ):
        for d in range(3):
            term = jnp.zeros((1, width), f32)
            for j in range(d + 1, 4):
                term = term + taps[3 - j] * tails[k][3 + d - j]
            out = jnp.where(place == d * REQ + k, term, out)
    return out


def first_tokens(shape, tok_dim, starts, ends):
    tok = iota(shape, tok_dim)
    place = iota(shape, 1 - tok_dim)
    out = jnp.zeros(shape, f32)
    for k in range(REQ):
        for d in range(3):
            hit = (place == d * REQ + k) & (tok == starts[k] + d) & (tok < ends[k])
            out = jnp.where(hit, 1.0, out)
    return out


def panel_kernel(w_ref, x_ref, bc_ref, out_ref):
    out_ref[:TOK, :] = w_ref[...]
    row = iota((16, CHAN), 0)
    wide = [
        bc_lanes(lambda block, i=i: bc_ref[i, :, pl.ds(pl.multiple_of(block * 128, 128), 128)])
        for i in range(3)
    ]
    for slot in range(REQ):
        value = jnp.zeros((16, CHAN), f32)
        for i in range(3):
            value = jnp.where(row == i, x_ref[i, slot : slot + 1, :], value)
            line = jnp.concatenate([wide[i][slot : slot + 1], jnp.zeros((1, 128), f32)], axis=1)
            value = jnp.where(row == 3 + i, line, value)
        out_ref[TOK + slot * 16 : TOK + (slot + 1) * 16, :] = value.astype(bf16)


def collect_kernel(mine_ref, b0, b1, b2, b3, out_ref):
    for k, ref in enumerate((b0, b1, b2, b3)):
        out_ref[k] = ref[...]


def collect(mine, value, rows, index, room):
    specs = [
        pl.BlockSpec((None, rows, CHAN), functools.partial(lambda k, i, m: index(m[k]), k))
        for k in range(REQ)
    ]
    return pl.pallas_call(
        collect_kernel,
        grid_spec=pltpu.PrefetchScalarGridSpec(
            num_scalar_prefetch=1,
            grid=(1,),
            in_specs=specs,
            out_specs=pl.BlockSpec(memory_space=pltpu.VMEM),
        ),
        out_shape=array(bf16, REQ, rows, CHAN),
        compiler_params=pltpu.CompilerParams(vmem_limit_bytes=room << 20),
        cost_estimate=pl.CostEstimate(flops=0, bytes_accessed=1 << 20, transcendentals=0),
    )(mine, value, value, value, value)


def place_kernel(plan, count, *refs):
    blocks, hz_ref, sems = refs[:count], refs[-2], refs[-1]
    copies = []
    for i, (step, low) in enumerate(plan):
        block = blocks[count - len(plan) + i]
        place = pl.multiple_of(((lax.axis_index("z") + step + 8) & 7) * CHAN, CHAN)
        target = hz_ref.at[low : low + block.shape[0], pl.ds(place, CHAN)]
        copies.append(pltpu.make_async_copy(block, target, sems.at[i]))
        copies[-1].start()
    for copy in copies:
        copy.wait()


def place_blocks(plan, operands):
    anywhere = pl.BlockSpec(memory_space=pl.ANY)
    return pl.pallas_call(
        functools.partial(place_kernel, plan, len(operands)),
        in_specs=[anywhere] * len(operands),
        out_specs=anywhere,
        out_shape=array(bf16, TOK, 8 * CHAN),
        input_output_aliases={0: 0} if len(operands) > len(plan) else {},
        scratch_shapes=[pltpu.SemaphoreType.DMA((len(plan),))],
        compiler_params=pltpu.CompilerParams(vmem_limit_bytes=4 << 20),
        cost_estimate=pl.CostEstimate(flops=0, bytes_accessed=1 << 20, transcendentals=0),
        name="place_blocks",
    )(*operands)


def small_kernel(hz_ref, wo_ref, wx_ref, out_ref):
    rows = hz_ref[...]
    core = lax.axis_index("core")
    for ref, place in ((wo_ref, core), (wx_ref, 1 - core)):
        cols = jnp.concatenate([ref[s] for s in range(8)], axis=1)
        out_ref[place] = lax.dot_general(cols, rows, NT, preferred_element_type=f32)


def conv_kernel(starts_ref, part_ref, tails_ref, taps_ref, bias_ref, bc_ref, dt_ref):
    starts, ends = bounds(starts_ref)
    signal = part_ref[0] + part_ref[1] + part_ref[2] + part_ref[3]
    dt_ref[...] = signal[64:]
    signal = signal[:64]
    own_taps = bc_lanes(lambda block: taps_ref[:, pl.ds(pl.multiple_of(block * 128, 128), 128)])
    own_bias = bc_lanes(lambda block: bias_ref[pl.ds(block, 1), :])
    taps = [own_taps[i : i + 1] for i in range(4)]
    tails = []
    for k in range(REQ):
        rows = tails_ref[k].astype(f32)
        tails.append([rows[3 + i : 4 + i, :128] for i in range(3)])
    table = jnp.concatenate(
        [
            tail_rows(tails, taps, 16, 128),
            own_taps,
            own_bias,
            jnp.zeros((107, 128), f32),
        ],
        axis=0,
    ).T
    onehot = first_tokens((128, TOK), 1, starts, ends)
    corr = jnp.dot(table, onehot, precision=HIGH, preferred_element_type=f32)[:64]
    tok = iota((64, TOK), 1)
    begin = own_start(tok, starts)
    summed = table[:64, 19:20] * signal + corr + table[:64, 20:21]
    for j in range(1, 4):
        moved = jnp.where(tok - j >= begin, pltpu.roll(signal, j, 1), 0.0)
        summed = summed + table[:64, 19 - j : 20 - j] * moved
    bc_ref[...] = sigmoid_gate(summed).astype(bf16)


def product(hz_ref, w_ref):
    panel = jnp.concatenate([w_ref[i, :TOK, :] for i in range(4)], axis=0)
    return jnp.dot(hz_ref[...], panel, preferred_element_type=f32)


def far_kernel(index_ref, hz_ref, w_ref, low_ref, high_ref):
    total = product(hz_ref, w_ref).astype(bf16)
    low_ref[...] = total[: TOK // 2]
    high_ref[...] = total[TOK // 2 :]


def own_kernel(index_ref, hz_ref, w_ref, out_ref):
    out_ref[...] = product(hz_ref, w_ref)


def near_kernel(low, index_ref, hz_ref, w_ref, add_ref, out_ref):
    total = product(hz_ref, w_ref)
    out_ref[...] = total.astype(bf16)
    rows = slice(low, low + TOK // 2)
    out_ref[rows, :] = (total[rows] + add_ref[...].astype(f32)).astype(bf16)


def partial(kernel, way, operands, outs):
    whole = pl.BlockSpec(memory_space=pltpu.VMEM)
    block = pl.BlockSpec((None, 4, BLOCK, CHAN), lambda i, b: ((b[0] + way) & 3, 0, 0, 0))
    index = lax.axis_index("yhi").astype(jnp.int32).reshape(1)
    return pl.pallas_call(
        kernel,
        grid_spec=pltpu.PrefetchScalarGridSpec(
            num_scalar_prefetch=1,
            grid=(1,),
            in_specs=[whole, block] + [whole] * (len(operands) - 2),
            out_specs=jax.tree.map(lambda _: whole, outs),
        ),
        out_shape=outs,
        compiler_params=pltpu.CompilerParams(vmem_limit_bytes=48 << 20),
        cost_estimate=pl.CostEstimate(
            flops=2 * 512 * 2048 * 256, bytes_accessed=3 << 20, transcendentals=0
        ),
    )(index, *operands)


def mixing_kernel(
    starts_ref, rate_ref, bias_ref, bc_ref, dt_ref, tails_ref, taps_ref,
    mix_ref, c_ref, cols_ref, decay_ref, b_ref, tail_ref,
):
    starts, ends = bounds(starts_ref)
    taps = [taps_ref[i : i + 1, :] for i in range(4)]
    tails = []
    for k in range(REQ):
        rows = tails_ref[k].astype(f32)
        tails.append([rows[i : i + 1, :] for i in range(3)])
    table = tail_rows(tails, taps, 128, CHAN)
    onehot = first_tokens((TOK, 128), 0, starts, ends)
    tail_ref[...] = jnp.dot(onehot, table, precision=HIGH, preferred_element_type=f32)
    b_rows = jnp.concatenate([bc_ref[s, 0:32, :] for s in range(8)], axis=0)
    c_rows = jnp.concatenate([bc_ref[s, 32:64, :] for s in range(8)], axis=0)
    b_ref[...] = b_rows
    c_cols = c_rows.astype(f32).T.astype(bf16)
    c_ref[...] = c_cols
    scores = jnp.dot(c_cols, b_rows, preferred_element_type=f32)

    row = iota((8, TOK), 0)
    tok = iota((8, TOK), 1)
    rate = jnp.zeros((8, TOK), f32)
    bias = jnp.zeros((8, TOK), f32)
    for h in range(HEAD_DEV):
        rate = jnp.where(row == h, rate_ref[h], rate)
        bias = jnp.where(row == h, bias_ref[h], bias)
    raw = dt_ref[0:8, :] + bias
    dt = jnp.maximum(raw, 0.0) + jnp.log1p(jnp.exp(-jnp.abs(raw)))
    decay = -rate * dt
    cum = decay
    step = 1
    while step < TOK:
        cum = cum + jnp.where(tok >= step, pltpu.roll(cum, step, 1), 0.0)
        step *= 2
    before = cum - decay
    at_start, at_end = [], []
    for k in range(REQ):
        first = jnp.minimum(starts[k], TOK - 1)
        at_start.append(jnp.sum(jnp.where(tok == first, before, 0.0), axis=1, keepdims=True))
        at_end.append(jnp.sum(jnp.where(tok == ends[k] - 1, cum, 0.0), axis=1, keepdims=True))
        decay_ref[k] = jnp.broadcast_to(jnp.exp(at_end[k] - at_start[k]), (8, 128))
    full_start = [jnp.broadcast_to(v, (8, TOK)) for v in at_start]
    full_end = [jnp.broadcast_to(v, (8, TOK)) for v in at_end]
    carried_decay = jnp.exp(cum - by_request(tok, starts, full_start))
    weight = jnp.exp(by_request(tok, starts, full_end) - cum) * dt
    cols = jnp.concatenate([cum, carried_decay, weight, jnp.zeros((104, TOK), f32)], axis=0).T
    cols_ref[...] = cols

    for b in range(4):
        low, width = b * 128, (b + 1) * 128
        tok_t = iota((128, width), 0) + low
        tok_s = iota((128, width), 1)
        inside = (tok_s <= tok_t) & (tok_s >= own_start(tok_t, starts))
        block = scores[low : low + 128, :width]
        for h in range(HEAD_DEV):
            gap = cols[low : low + 128, h : h + 1] - cum[h : h + 1, :width]
            grown = jnp.exp(jnp.where(inside, gap, 0.0))
            value = jnp.where(inside, block * grown * dt[h : h + 1, :width], 0.0)
            mix_ref[h, low : low + 128, 0:width] = value.astype(bf16)


def output_kernel(
    starts_ref, count_ref, skip_ref, x0, x1, x2, served_ref, taps_ref, bias_ref,
    mix_ref, c_ref, cols_ref, decay_ref, b_ref, tail_ref, y_ref, state_ref,
):
    starts, ends = bounds(starts_ref)
    count = count_ref[group_index()]
    signal = x0[...] + x1[...].astype(f32) + x2[...].astype(f32)
    taps = [taps_ref[i : i + 1, :] for i in range(4)]
    bias = jnp.concatenate([bias_ref[0:1, :], bias_ref[1:2, :]], axis=1)
    summed = tail_ref[...]
    tok = iota((TOK, CHAN), 0)
    lane = iota((TOK, CHAN), 1)
    begin = own_start(tok, starts)
    summed = summed + taps[3] * signal + bias
    for j in range(1, 4):
        moved = jnp.where(tok - j >= begin, pltpu.roll(signal, j, 0), 0.0)
        summed = summed + taps[3 - j] * moved
    x_low = sigmoid_gate(summed).astype(bf16)
    x_wide = x_low.astype(f32)
    skip = jnp.zeros((TOK, CHAN), f32)
    for h in range(HEAD_DEV):
        skip = jnp.where(lane >= h * P_SIZE, skip_ref[h], skip)
    carry = jnp.zeros((TOK, CHAN), f32)
    scale = jnp.zeros((TOK, CHAN), f32)
    for k in range(REQ):
        part = lax.dot_general(c_ref[...], served_ref[k], NT, preferred_element_type=f32)
        carry = jnp.where((tok >= starts[k]) & (tok < ends[k]), part, carry)
    for h in range(HEAD_DEV):
        scale = jnp.where(lane >= h * P_SIZE, cols_ref[:, 8 + h : 9 + h], scale)
    base = carry * scale + skip * x_wide
    for b in range(4):
        low, width = b * 128, (b + 1) * 128
        total = base[low : low + 128]
        for h in range(HEAD_DEV):
            mine = (lane[:width] >= h * P_SIZE) & (lane[:width] < (h + 1) * P_SIZE)
            x_head = jnp.where(mine, x_wide[:width], 0.0).astype(bf16)
            total = total + jnp.dot(
                mix_ref[h, low : low + 128, 0:width], x_head, preferred_element_type=f32
            )
        y_ref[low : low + 128, :] = total.astype(bf16)

    weight = jnp.zeros((TOK, CHAN), f32)
    for h in range(HEAD_DEV):
        weight = jnp.where(lane >= h * P_SIZE, cols_ref[:, 16 + h : 17 + h], weight)
    weighted = (x_wide * weight).T
    high = weighted.astype(bf16).astype(f32)
    rest = weighted - high
    tok_r = iota((CHAN, TOK), 1)
    b_rows = b_ref[...]
    for k in range(REQ):
        member = (tok_r >= starts[k]) & (tok_r < ends[k])
        gained = lax.dot_general(
            jnp.where(member, high, 0.0).astype(bf16), b_rows, NT, preferred_element_type=f32
        ) + lax.dot_general(
            jnp.where(member, rest, 0.0).astype(bf16), b_rows, NT, preferred_element_type=f32
        )
        for h in range(HEAD_DEV):
            lo, hi = h * P_SIZE, (h + 1) * P_SIZE
            old = served_ref[k, lo:hi, :].astype(f32)
            new = decay_ref[k, h : h + 1, 0:1] * old + gained[lo:hi]
            state_ref[k, lo:hi, :] = jnp.where(k < count, new, 0.0)


def layer(
    hidden, w_x, w_small, conv_x, conv_x_bias, conv_bc, conv_bc_bias, rate, dt_bias, dskip,
    old_state, x_tail, bc_tail, req_count, req_source, req_start,
):
    core = lax.axis_index("core")
    starts = req_start.T
    mine = lax.dynamic_index_in_dim(req_source, lax.axis_index(GROUP), 0, keepdims=False)

    swap = [(a * 4 + b, b * 4 + a) for a in range(4) for b in range(4)]
    w_swapped = lax.ppermute(w_x, ("x", "yhi"), swap)
    panel = call(
        panel_kernel,
        (),
        (w_swapped, x_tail.transpose(1, 0, 2), bc_tail.transpose(1, 0, 2)),
        array(bf16, BLOCK, CHAN),
        moved=1 << 20,
    )
    w_all = lax.all_gather(panel, GROUP, axis=0, tiled=False)
    tails = collect(mine, w_all, 16, lambda m: (m >> 2, 32 + (m & 3), 0), 55)

    up = [(i, (i + 1) % 8) for i in range(8)]
    down = [(i, (i - 1) % 8) for i in range(8)]
    blocks = [hidden]
    for ring in (up, down):
        block = hidden
        for _ in range(3):
            block = lax.ppermute(block, "z", ring)
            blocks.append(block)
    half = TOK // 2
    blocks.append(lax.ppermute(blocks[3][:half], "z", up))
    blocks.append(lax.ppermute(blocks[6][half:], "z", down))

    w_t = w_small.T
    w_b = w_t[:1024].reshape(4, 8, 32, 256)
    w_c = w_t[1024:2048].reshape(4, 8, 32, 256)
    w_d = jnp.pad(w_t[2048:].reshape(4, 8, 4, 256), ((0, 0), (0, 0), (0, SMALL - 68), (0, 0)))
    w_cols = jnp.concatenate([w_b, w_c, w_d], axis=2)
    w_cols = lax.dynamic_slice_in_dim(w_cols, core * 2, 2, 0)
    w_cols = w_cols.transpose(1, 0, 2, 3).reshape(8, 2 * SMALL, 256)
    w_cols = lax.all_to_all(w_cols, "z", 0, 0, tiled=True)
    w_other = lax.ppermute(w_cols, "core", [(0, 1), (1, 0)])

    states = old_state.reshape(REQ, CHAN, STATES).astype(bf16)
    states = lax.all_gather(states, GROUP, axis=0, tiled=True)
    served = collect(mine, states, CHAN, lambda m: (m, 0, 0), 53)

    hz = place_blocks(((0, 0), (-1, 0), (1, 0)), (hidden, blocks[1], blocks[4]))
    for step in (2, 3):
        hz = place_blocks(((-step, 0), (step, 0)), (hz, blocks[step], blocks[step + 3]))
    hz = place_blocks(((4, 0), (4, half)), (hz, blocks[7], blocks[8]))
    part_small = call(
        small_kernel,
        (),
        (hz, w_cols, w_other),
        array(f32, 2, 2 * SMALL, TOK),
        flops=2 * 288 * 2048 * 512,
        moved=4 << 20,
    )
    part_small = lax.all_to_all(part_small.reshape(4, SMALL, TOK), "yhi", 0, 0, tiled=True)

    bc_own, dt_raw = call(
        conv_kernel,
        (starts,),
        (part_small, tails, conv_bc, conv_bc_bias.reshape(16, 128)),
        (array(bf16, 64, TOK), array(f32, SMALL - 64, TOK)),
        flops=2 * 6 * 128 * 128 * 512,
        moved=1 << 20,
    )
    bc_all = lax.all_to_all(
        jnp.broadcast_to(bc_own[None], (8, 64, TOK)), "z", 0, 0, tiled=True
    )

    w_view = w_all.reshape(4, 4, BLOCK, CHAN)
    ahead = [(i, (i + 1) % 4) for i in range(4)]
    back = [(i, (i - 1) % 4) for i in range(4)]
    low, high = partial(far_kernel, 2, (hz, w_view), (array(bf16, half, CHAN),) * 2)
    low = lax.ppermute(low, "yhi", ahead)
    high = lax.ppermute(high, "yhi", back)
    x0 = partial(own_kernel, 0, (hz, w_view), array(f32, TOK, CHAN))
    x1 = partial(
        functools.partial(near_kernel, 0),
        1, (hz, w_view, low), array(bf16, TOK, CHAN),
    )
    x1 = lax.ppermute(x1, "yhi", ahead)
    x2 = partial(
        functools.partial(near_kernel, half),
        3, (hz, w_view, high), array(bf16, TOK, CHAN),
    )
    x2 = lax.ppermute(x2, "yhi", back)

    made = call(
        mixing_kernel,
        (starts, rate, dt_bias),
        (bc_all, dt_raw, tails, conv_x),
        (
            array(bf16, HEAD_DEV, TOK, TOK),
            array(bf16, TOK, STATES),
            array(f32, TOK, 128),
            array(f32, REQ, 8, 128),
            array(bf16, STATES, TOK),
            array(f32, TOK, CHAN),
        ),
        flops=2 * 8 * 512 * 256 * 256,
        moved=12 << 20,
        room=24,
    )
    y, state = call(
        output_kernel,
        (starts, req_count, dskip),
        (x0, x1, x2, served, conv_x, conv_x_bias.reshape(2, 128), *made),
        (array(bf16, TOK, CHAN), array(f32, REQ, 256, STATES)),
        flops=2 * 20 * 512 * 256 * 256,
        moved=6 << 20,
        room=24,
    )
    return y, state.reshape(REQ, HEAD_DEV, P_SIZE, STATES)


def solution(mesh):
    fine = jax.sharding.Mesh(mesh.devices.reshape(4, 2, 2, 4, 8), ("x", "ylo", "core", "yhi", "z"))
    g, s = GROUP, SHARD
    in_specs = (
        P(g, s),
        P(g, s),
        P(s, None),
        P(None, s),
        P(s),
        P(),
        P(),
        P(s),
        P(s),
        P(s),
        P(g, s, None, None),
        P(g, None, s),
        P(g, None, None),
        P(),
        P(),
        P(),
    )
    out_specs = (P(g, s), P(g, s, None, None))
    return jax.shard_map(layer, mesh=fine, in_specs=in_specs, out_specs=out_specs, check_vma=False)
```

```python
import functools

import jax
import jax.numpy as jnp
from jax import lax
from jax.experimental import pallas as pl
from jax.experimental.pallas import tpu as pltpu
from jax.sharding import PartitionSpec as P


TOK = 512
STATES = 256
CHAN = 256
HEAD_DEV = 4
P_SIZE = 64
REQ = 4
GROUPS = 16
GROUP = ("x", "ylo", "core")
SHARD = ("yhi", "z")
SMALL = 72
BLOCK = 576
SPLIT = 192


bf16 = jnp.bfloat16
f32 = jnp.float32
NT = (((1,), (1,)), ((), ()))
HIGH = lax.Precision.HIGHEST


def iota(shape, dim):
    return lax.broadcasted_iota(jnp.int32, shape, dim)


def call(kernel, scalars, operands, outs, flops=0, moved=0, scratch=(), room=8):
    smem = pl.BlockSpec(memory_space=pltpu.SMEM)
    whole = pl.BlockSpec(memory_space=pltpu.VMEM)
    return pl.pallas_call(
        kernel,
        in_specs=[smem] * len(scalars) + [whole] * len(operands),
        out_specs=jax.tree.map(lambda _: whole, outs),
        out_shape=outs,
        scratch_shapes=scratch,
        compiler_params=pltpu.CompilerParams(vmem_limit_bytes=room << 20),
        cost_estimate=pl.CostEstimate(flops=flops, bytes_accessed=moved, transcendentals=0),
    )(*scalars, *operands)


def array(dtype, *shape):
    return jax.ShapeDtypeStruct(shape, dtype)


def group_index():
    return lax.axis_index("x") * 4 + lax.axis_index("ylo") * 2 + lax.axis_index("core")


def bounds(starts_ref):
    group = group_index()
    starts = [starts_ref[k, group] for k in range(REQ)]
    ends = [jnp.minimum(s, TOK) for s in starts[1:]] + [jnp.int32(TOK)]
    return starts, ends


def bc_lanes(read):
    yhi, z = lax.axis_index("yhi"), lax.axis_index("z")
    block, offset = yhi * 2 + (z >> 2), (z & 3) * 32
    b = pltpu.roll(read(block), (128 - offset) & 127, 1)
    c = pltpu.roll(read(block + 8), (160 - offset) & 127, 1)
    lane = iota(b.shape, 1)
    return jnp.where(lane < 32, b, jnp.where(lane < 64, c, 0.0))


def own_start(tok, starts):
    out = jnp.zeros_like(tok)
    for k in range(1, REQ):
        out = jnp.where(tok >= starts[k], starts[k], out)
    return out


def by_request(tok, starts, values):
    out = values[0]
    for k in range(1, REQ):
        out = jnp.where(tok >= starts[k], values[k], out)
    return out


def sigmoid_gate(v):
    return v * jax.nn.sigmoid(v)


def tail_rows(tails, taps, rows, width):
    place = iota((rows, width), 0)
    out = jnp.zeros((rows, width), f32)
    for k in range(REQ):
        for d in range(3):
            term = jnp.zeros((1, width), f32)
            for j in range(d + 1, 4):
                term = term + taps[3 - j] * tails[k][3 + d - j]
            out = jnp.where(place == d * REQ + k, term, out)
    return out


def first_tokens(shape, tok_dim, starts, ends):
    tok = iota(shape, tok_dim)
    place = iota(shape, 1 - tok_dim)
    out = jnp.zeros(shape, f32)
    for k in range(REQ):
        for d in range(3):
            hit = (place == d * REQ + k) & (tok == starts[k] + d) & (tok < ends[k])
            out = jnp.where(hit, 1.0, out)
    return out


def slot_for(src_ref, target):
    group = group_index()
    slot = jnp.int32(0)
    for k in range(REQ):
        place = src_ref[k, target]
        slot = jnp.where((place >> 2) == group, place & 3, slot)
    return slot


def pack_kernel(src_ref, state_ref, out_ref):
    @pl.loop(0, GROUPS)
    def _(i):
        out_ref[i] = state_ref[slot_for(src_ref, i), :SPLIT, :].astype(bf16)


def panel_kernel(w_ref, x_ref, bc_ref, out_ref):
    out_ref[:TOK, :] = w_ref[...]
    row = iota((16, CHAN), 0)
    wide = [
        bc_lanes(lambda block, i=i: bc_ref[i, :, pl.ds(pl.multiple_of(block * 128, 128), 128)])
        for i in range(3)
    ]
    for slot in range(REQ):
        value = jnp.zeros((16, CHAN), f32)
        for i in range(3):
            value = jnp.where(row == i, x_ref[i, slot : slot + 1, :], value)
            line = jnp.concatenate([wide[i][slot : slot + 1], jnp.zeros((1, 128), f32)], axis=1)
            value = jnp.where(row == 3 + i, line, value)
        out_ref[TOK + slot * 16 : TOK + (slot + 1) * 16, :] = value.astype(bf16)


def collect_kernel(mine_ref, b0, b1, b2, b3, out_ref):
    for k, ref in enumerate((b0, b1, b2, b3)):
        out_ref[k] = ref[...]


def collect(mine, value, rows, index, room):
    specs = [
        pl.BlockSpec((None, rows, CHAN), functools.partial(lambda k, i, m: index(m[k]), k))
        for k in range(REQ)
    ]
    return pl.pallas_call(
        collect_kernel,
        grid_spec=pltpu.PrefetchScalarGridSpec(
            num_scalar_prefetch=1,
            grid=(1,),
            in_specs=specs,
            out_specs=pl.BlockSpec(memory_space=pltpu.VMEM),
        ),
        out_shape=array(bf16, REQ, rows, CHAN),
        compiler_params=pltpu.CompilerParams(vmem_limit_bytes=room << 20),
        cost_estimate=pl.CostEstimate(flops=0, bytes_accessed=1 << 20, transcendentals=0),
    )(mine, value, value, value, value)


def place_kernel(plan, count, *refs):
    blocks, hz_ref, sems = refs[:count], refs[-2], refs[-1]
    copies = []
    for i, (step, low) in enumerate(plan):
        block = blocks[count - len(plan) + i]
        place = pl.multiple_of(((lax.axis_index("z") + step + 8) & 7) * CHAN, CHAN)
        target = hz_ref.at[low : low + block.shape[0], pl.ds(place, CHAN)]
        copies.append(pltpu.make_async_copy(block, target, sems.at[i]))
        copies[-1].start()
    for copy in copies:
        copy.wait()


def place_blocks(plan, operands):
    anywhere = pl.BlockSpec(memory_space=pl.ANY)
    return pl.pallas_call(
        functools.partial(place_kernel, plan, len(operands)),
        in_specs=[anywhere] * len(operands),
        out_specs=anywhere,
        out_shape=array(bf16, TOK, 8 * CHAN),
        input_output_aliases={0: 0} if len(operands) > len(plan) else {},
        scratch_shapes=[pltpu.SemaphoreType.DMA((len(plan),))],
        compiler_params=pltpu.CompilerParams(vmem_limit_bytes=4 << 20),
        cost_estimate=pl.CostEstimate(flops=0, bytes_accessed=1 << 20, transcendentals=0),
        name="place_blocks",
    )(*operands)


def small_kernel(hz_ref, wo_ref, wx_ref, out_ref):
    rows = hz_ref[...]
    core = lax.axis_index("core")
    for ref, place in ((wo_ref, core), (wx_ref, 1 - core)):
        cols = jnp.concatenate([ref[s] for s in range(8)], axis=1)
        out_ref[place] = lax.dot_general(cols, rows, NT, preferred_element_type=f32)


def conv_kernel(starts_ref, part_ref, tails_ref, taps_ref, bias_ref, bc_ref, dt_ref):
    starts, ends = bounds(starts_ref)
    signal = part_ref[0] + part_ref[1] + part_ref[2] + part_ref[3]
    dt_ref[...] = signal[64:]
    signal = signal[:64]
    own_taps = bc_lanes(lambda block: taps_ref[:, pl.ds(pl.multiple_of(block * 128, 128), 128)])
    own_bias = bc_lanes(lambda block: bias_ref[pl.ds(block, 1), :])
    taps = [own_taps[i : i + 1] for i in range(4)]
    tails = []
    for k in range(REQ):
        rows = tails_ref[k].astype(f32)
        tails.append([rows[3 + i : 4 + i, :128] for i in range(3)])
    table = jnp.concatenate(
        [
            tail_rows(tails, taps, 16, 128),
            own_taps,
            own_bias,
            jnp.zeros((107, 128), f32),
        ],
        axis=0,
    ).T
    onehot = first_tokens((128, TOK), 1, starts, ends)
    corr = jnp.dot(table, onehot, precision=HIGH, preferred_element_type=f32)[:64]
    tok = iota((64, TOK), 1)
    begin = own_start(tok, starts)
    summed = table[:64, 19:20] * signal + corr + table[:64, 20:21]
    for j in range(1, 4):
        moved = jnp.where(tok - j >= begin, pltpu.roll(signal, j, 1), 0.0)
        summed = summed + table[:64, 19 - j : 20 - j] * moved
    mine = sigmoid_gate(summed).astype(bf16)
    for i in range(8):
        bc_ref[i] = mine


def product(hz_ref, w_ref):
    panel = jnp.concatenate([w_ref[i, :TOK, :] for i in range(4)], axis=0)
    return jnp.dot(hz_ref[...], panel, preferred_element_type=f32)


def far_kernel(index_ref, hz_ref, w_ref, low_ref, high_ref):
    total = product(hz_ref, w_ref).astype(bf16)
    low_ref[...] = total[: TOK // 2]
    high_ref[...] = total[TOK // 2 :]


def own_kernel(index_ref, hz_ref, w_ref, out_ref):
    out_ref[...] = product(hz_ref, w_ref)


def near_kernel(low, index_ref, hz_ref, w_ref, add_ref, out_ref):
    total = product(hz_ref, w_ref)
    out_ref[...] = total.astype(bf16)
    rows = slice(low, low + TOK // 2)
    out_ref[rows, :] = (total[rows] + add_ref[...].astype(f32)).astype(bf16)


def partial(kernel, way, operands, outs):
    whole = pl.BlockSpec(memory_space=pltpu.VMEM)
    block = pl.BlockSpec((None, 4, BLOCK, CHAN), lambda i, b: ((b[0] + way) & 3, 0, 0, 0))
    index = lax.axis_index("yhi").astype(jnp.int32).reshape(1)
    return pl.pallas_call(
        kernel,
        grid_spec=pltpu.PrefetchScalarGridSpec(
            num_scalar_prefetch=1,
            grid=(1,),
            in_specs=[whole, block] + [whole] * (len(operands) - 2),
            out_specs=jax.tree.map(lambda _: whole, outs),
        ),
        out_shape=outs,
        compiler_params=pltpu.CompilerParams(vmem_limit_bytes=48 << 20),
        cost_estimate=pl.CostEstimate(
            flops=2 * 512 * 2048 * 256, bytes_accessed=3 << 20, transcendentals=0
        ),
    )(index, *operands)


def mixing_kernel(
    starts_ref, rate_ref, bias_ref, bc_ref, dt_ref, tails_ref, taps_ref,
    mix_ref, c_ref, cols_ref, decay_ref, b_ref, tail_ref,
):
    starts, ends = bounds(starts_ref)
    taps = [taps_ref[i : i + 1, :] for i in range(4)]
    tails = []
    for k in range(REQ):
        rows = tails_ref[k].astype(f32)
        tails.append([rows[i : i + 1, :] for i in range(3)])
    table = tail_rows(tails, taps, 128, CHAN)
    onehot = first_tokens((TOK, 128), 0, starts, ends)
    tail_ref[...] = jnp.dot(onehot, table, precision=HIGH, preferred_element_type=f32)
    b_rows = jnp.concatenate([bc_ref[s, 0:32, :] for s in range(8)], axis=0)
    c_rows = jnp.concatenate([bc_ref[s, 32:64, :] for s in range(8)], axis=0)
    b_ref[...] = b_rows
    c_cols = c_rows.astype(f32).T.astype(bf16)
    c_ref[...] = c_cols
    scores = jnp.dot(c_cols, b_rows, preferred_element_type=f32)

    row = iota((8, TOK), 0)
    tok = iota((8, TOK), 1)
    rate = jnp.zeros((8, TOK), f32)
    bias = jnp.zeros((8, TOK), f32)
    for h in range(HEAD_DEV):
        rate = jnp.where(row == h, rate_ref[h], rate)
        bias = jnp.where(row == h, bias_ref[h], bias)
    raw = dt_ref[0:8, :] + bias
    dt = jnp.maximum(raw, 0.0) + jnp.log1p(jnp.exp(-jnp.abs(raw)))
    decay = -rate * dt
    cum = decay
    step = 1
    while step < TOK:
        cum = cum + jnp.where(tok >= step, pltpu.roll(cum, step, 1), 0.0)
        step *= 2
    before = cum - decay
    at_start, at_end = [], []
    for k in range(REQ):
        first = jnp.minimum(starts[k], TOK - 1)
        at_start.append(jnp.sum(jnp.where(tok == first, before, 0.0), axis=1, keepdims=True))
        at_end.append(jnp.sum(jnp.where(tok == ends[k] - 1, cum, 0.0), axis=1, keepdims=True))
        decay_ref[k] = jnp.broadcast_to(jnp.exp(at_end[k] - at_start[k]), (8, 128))
    full_start = [jnp.broadcast_to(v, (8, TOK)) for v in at_start]
    full_end = [jnp.broadcast_to(v, (8, TOK)) for v in at_end]
    carried_decay = jnp.exp(cum - by_request(tok, starts, full_start))
    weight = jnp.exp(by_request(tok, starts, full_end) - cum) * dt
    cols = jnp.concatenate([cum, carried_decay, weight, jnp.zeros((104, TOK), f32)], axis=0).T
    cols_ref[...] = cols

    for b in range(4):
        low, width = b * 128, (b + 1) * 128
        tok_t = iota((128, width), 0) + low
        tok_s = iota((128, width), 1)
        inside = (tok_s <= tok_t) & (tok_s >= own_start(tok_t, starts))
        block = scores[low : low + 128, :width]
        for h in range(HEAD_DEV):
            gap = cols[low : low + 128, h : h + 1] - cum[h : h + 1, :width]
            grown = jnp.exp(jnp.where(inside, gap, 0.0))
            value = jnp.where(inside, block * grown * dt[h : h + 1, :width], 0.0)
            mix_ref[h, low : low + 128, 0:width] = value.astype(bf16)


def output_kernel(
    starts_ref, src_ref, count_ref, skip_ref, x0, x1, x2, early_ref, served_ref, taps_ref, bias_ref,
    mix_ref, c_ref, cols_ref, decay_ref, b_ref, tail_ref, y_ref, state_ref,
):
    starts, ends = bounds(starts_ref)
    count = count_ref[group_index()]
    signal = x0[...] + x1[...].astype(f32) + x2[...].astype(f32)
    taps = [taps_ref[i : i + 1, :] for i in range(4)]
    bias = jnp.concatenate([bias_ref[0:1, :], bias_ref[1:2, :]], axis=1)
    summed = tail_ref[...]
    tok = iota((TOK, CHAN), 0)
    lane = iota((TOK, CHAN), 1)
    begin = own_start(tok, starts)
    summed = summed + taps[3] * signal + bias
    for j in range(1, 4):
        moved = jnp.where(tok - j >= begin, pltpu.roll(signal, j, 0), 0.0)
        summed = summed + taps[3 - j] * moved
    x_low = sigmoid_gate(summed).astype(bf16)
    x_wide = x_low.astype(f32)
    skip = jnp.zeros((TOK, CHAN), f32)
    for h in range(HEAD_DEV):
        skip = jnp.where(lane >= h * P_SIZE, skip_ref[h], skip)
    carry = jnp.zeros((TOK, CHAN), f32)
    scale = jnp.zeros((TOK, CHAN), f32)
    for k in range(REQ):
        old = (early_ref[src_ref[k, group_index()] >> 2], served_ref[k])
        part = jnp.concatenate(
            [lax.dot_general(c_ref[...], v, NT, preferred_element_type=f32) for v in old], axis=1
        )
        carry = jnp.where((tok >= starts[k]) & (tok < ends[k]), part, carry)
    for h in range(HEAD_DEV):
        scale = jnp.where(lane >= h * P_SIZE, cols_ref[:, 8 + h : 9 + h], scale)
    base = carry * scale + skip * x_wide
    for b in range(4):
        low, width = b * 128, (b + 1) * 128
        total = base[low : low + 128]
        for h in range(HEAD_DEV):
            mine = (lane[:width] >= h * P_SIZE) & (lane[:width] < (h + 1) * P_SIZE)
            x_head = jnp.where(mine, x_wide[:width], 0.0).astype(bf16)
            total = total + jnp.dot(
                mix_ref[h, low : low + 128, 0:width], x_head, preferred_element_type=f32
            )
        y_ref[low : low + 128, :] = total.astype(bf16)

    weight = jnp.zeros((TOK, CHAN), f32)
    for h in range(HEAD_DEV):
        weight = jnp.where(lane >= h * P_SIZE, cols_ref[:, 16 + h : 17 + h], weight)
    weighted = (x_wide * weight).T
    high = weighted.astype(bf16).astype(f32)
    rest = weighted - high
    tok_r = iota((CHAN, TOK), 1)
    b_rows = b_ref[...]
    for k in range(REQ):
        member = (tok_r >= starts[k]) & (tok_r < ends[k])
        gained = lax.dot_general(
            jnp.where(member, high, 0.0).astype(bf16), b_rows, NT, preferred_element_type=f32
        ) + lax.dot_general(
            jnp.where(member, rest, 0.0).astype(bf16), b_rows, NT, preferred_element_type=f32
        )
        for h in range(HEAD_DEV):
            lo, hi = h * P_SIZE, (h + 1) * P_SIZE
            if hi <= SPLIT:
                old = early_ref[src_ref[k, group_index()] >> 2, lo:hi, :].astype(f32)
            else:
                old = served_ref[k, lo - SPLIT : hi - SPLIT, :].astype(f32)
            new = decay_ref[k, h : h + 1, 0:1] * old + gained[lo:hi]
            state_ref[k, lo:hi, :] = jnp.where(k < count, new, 0.0)


def layer(
    hidden, w_x, w_small, conv_x, conv_x_bias, conv_bc, conv_bc_bias, rate, dt_bias, dskip,
    old_state, x_tail, bc_tail, req_count, req_source, req_start,
):
    core = lax.axis_index("core")
    src, starts = req_source.T, req_start.T
    mine = lax.dynamic_index_in_dim(req_source, lax.axis_index(GROUP), 0, keepdims=False)

    swap = [(a * 4 + b, b * 4 + a) for a in range(4) for b in range(4)]
    w_swapped = lax.ppermute(w_x, ("x", "yhi"), swap)
    panel = call(
        panel_kernel,
        (),
        (w_swapped, x_tail.transpose(1, 0, 2), bc_tail.transpose(1, 0, 2)),
        array(bf16, BLOCK, CHAN),
        moved=1 << 20,
    )
    w_all = lax.all_gather(panel, GROUP, axis=0, tiled=False)
    tails = collect(mine, w_all, 16, lambda m: (m >> 2, 32 + (m & 3), 0), 55)

    up = [(i, (i + 1) % 8) for i in range(8)]
    down = [(i, (i - 1) % 8) for i in range(8)]
    blocks = [hidden]
    for ring in (up, down):
        block = hidden
        for _ in range(3):
            block = lax.ppermute(block, "z", ring)
            blocks.append(block)
    half = TOK // 2
    blocks.append(lax.ppermute(blocks[3][:half], "z", up))
    blocks.append(lax.ppermute(blocks[6][half:], "z", down))

    w_t = w_small.T
    w_b = w_t[:1024].reshape(4, 8, 32, 256)
    w_c = w_t[1024:2048].reshape(4, 8, 32, 256)
    w_d = jnp.pad(w_t[2048:].reshape(4, 8, 4, 256), ((0, 0), (0, 0), (0, SMALL - 68), (0, 0)))
    w_cols = jnp.concatenate([w_b, w_c, w_d], axis=2)
    w_cols = lax.dynamic_slice_in_dim(w_cols, core * 2, 2, 0)
    w_cols = w_cols.transpose(1, 0, 2, 3).reshape(8, 2 * SMALL, 256)
    w_cols = lax.all_to_all(w_cols, "z", 0, 0, tiled=True)
    w_other = lax.ppermute(w_cols, "core", [(0, 1), (1, 0)])

    states = old_state.reshape(REQ, CHAN, STATES)
    early = call(pack_kernel, (src,), (states,), array(bf16, GROUPS, SPLIT, STATES), moved=4 << 20)
    early = lax.all_to_all(early, GROUP, 0, 0, tiled=True)
    states = lax.all_gather(states[:, SPLIT:].astype(bf16), GROUP, axis=0, tiled=True)
    served = collect(mine, states, CHAN - SPLIT, lambda m: (m, 0, 0), 55)

    hz = place_blocks(((0, 0), (-1, 0), (1, 0)), (hidden, blocks[1], blocks[4]))
    for step in (2, 3):
        hz = place_blocks(((-step, 0), (step, 0)), (hz, blocks[step], blocks[step + 3]))
    hz = place_blocks(((4, 0), (4, half)), (hz, blocks[7], blocks[8]))
    part_small = call(
        small_kernel,
        (),
        (hz, w_cols, w_other),
        array(f32, 2, 2 * SMALL, TOK),
        flops=2 * 288 * 2048 * 512,
        moved=4 << 20,
    )
    part_small = lax.all_to_all(part_small.reshape(4, SMALL, TOK), "yhi", 0, 0, tiled=True)

    bc_own, dt_raw = call(
        conv_kernel,
        (starts,),
        (part_small, tails, conv_bc, conv_bc_bias.reshape(16, 128)),
        (array(bf16, 8, 64, TOK), array(f32, SMALL - 64, TOK)),
        flops=2 * 6 * 128 * 128 * 512,
        moved=1 << 20,
    )
    bc_all = lax.all_to_all(bc_own, "z", 0, 0, tiled=True)

    w_view = w_all.reshape(4, 4, BLOCK, CHAN)
    ahead = [(i, (i + 1) % 4) for i in range(4)]
    back = [(i, (i - 1) % 4) for i in range(4)]
    low, high = partial(far_kernel, 2, (hz, w_view), (array(bf16, half, CHAN),) * 2)
    low = lax.ppermute(low, "yhi", ahead)
    high = lax.ppermute(high, "yhi", back)
    x0 = partial(own_kernel, 0, (hz, w_view), array(f32, TOK, CHAN))
    x1 = partial(
        functools.partial(near_kernel, 0),
        1, (hz, w_view, low), array(bf16, TOK, CHAN),
    )
    x1 = lax.ppermute(x1, "yhi", ahead)
    x2 = partial(
        functools.partial(near_kernel, half),
        3, (hz, w_view, high), array(bf16, TOK, CHAN),
    )
    x2 = lax.ppermute(x2, "yhi", back)

    made = call(
        mixing_kernel,
        (starts, rate, dt_bias),
        (bc_all, dt_raw, tails, conv_x),
        (
            array(bf16, HEAD_DEV, TOK, TOK),
            array(bf16, TOK, STATES),
            array(f32, TOK, 128),
            array(f32, REQ, 8, 128),
            array(bf16, STATES, TOK),
            array(f32, TOK, CHAN),
        ),
        flops=2 * 8 * 512 * 256 * 256,
        moved=12 << 20,
        room=24,
    )
    y, state = call(
        output_kernel,
        (starts, src, req_count, dskip),
        (x0, x1, x2, early, served, conv_x, conv_x_bias.reshape(2, 128), *made),
        (array(bf16, TOK, CHAN), array(f32, REQ, 256, STATES)),
        flops=2 * 20 * 512 * 256 * 256,
        moved=6 << 20,
        room=24,
    )
    return y, state.reshape(REQ, HEAD_DEV, P_SIZE, STATES)


def solution(mesh):
    fine = jax.sharding.Mesh(mesh.devices.reshape(4, 2, 2, 4, 8), ("x", "ylo", "core", "yhi", "z"))
    g, s = GROUP, SHARD
    in_specs = (
        P(g, s),
        P(g, s),
        P(s, None),
        P(None, s),
        P(s),
        P(),
        P(),
        P(s),
        P(s),
        P(s),
        P(g, s, None, None),
        P(g, None, s),
        P(g, None, None),
        P(),
        P(),
        P(),
    )
    out_specs = (P(g, s), P(g, s, None, None))
    return jax.shard_map(layer, mesh=fine, in_specs=in_specs, out_specs=out_specs, check_vma=False)
```
